512 devices in a mesh: grp: 16 (over y, core), col: 32 (over x, z).
Axes of the slice: x: 4, y: 8, z: 8, core: 2. Of those that a mesh axis runs over, the one named last changes fastest.
Arguments:
- conc: float32 [12, 256, 65536], P(None, 'col', 'grp'), may hold values from 0.1 to 10
- porosity: float32 [256, 65536], P('col', 'grp'), may hold values from 0.2 to 0.5
- cell_cond: float32 [256, 65536], P('col', 'grp'), may hold values from 0.5 to 2
- soil_class: int32 [65536], P(('grp', 'col')), may hold values from 0 to 15
- active: int32 [65536], P(('grp', 'col')), may hold values from 64 to 256
- class_cond: float32 [16], replicated, may hold values from 20 to 400
- sorb_affinity: float32 [16, 12], replicated, may hold values from 0.05 to 5
- sorb_capacity: float32 [16], replicated, may hold values from 1 to 20
- surf_conc: float32 [12, 262144], P(None, ('grp', 'col')), may hold values from 0.1 to 10
- surf_rate: float32 [262144], P(('grp', 'col')), may hold values from 0.1 to 2
- surf_group: int32 [262144, 1], P(('grp', 'col')), may hold values from 0 to 15; in each aligned block of 512 rows (0 to 511, 512 to 1023, ...) at most 128 rows name the same one
- surf_local: int32 [262144], P(('grp', 'col')), may hold values from 0 to 127
Outputs:
- log_free: float32 [12, 256, 65536], P(None, 'col', 'grp')
- surf_flux: float32 [12, 262144], P(None, ('grp', 'col'))
The draws below stay inside these ranges and needn't reach their ends.
Inputs may be any that keep to these rules, and one draw needn't show every extreme that they name: `surf_group`: among the rows of one device (aligned blocks of 512 rows) at most 128 name the same group, a bound that some block reaches of one device.
All inputs are finite; a program needn't handle non-finite values.
Results may differ from the reference program's by a relative error of at most 0.0003.
Values sent between devices are 32-bit elements; how exact they have to be, the bound alone decides.
No kernel may reach another device: no remote copies, remote signals or barrier semaphores. Data moves between devices by JAX's collectives and lax.ppermute only.
A program may use at most 128 MiB of HBM per device.

```python
import math
import jax
import jax.numpy as jnp
import numpy as np
from jax import lax

NC = 12
LAYERS = 256
NCLASS = 16
ITERS = 4
COL_DEV = 128
SURF_DEV = 512
CAP = 128
GROUPS = 16
GC = 4096
COLUMNS = 65536
SURF = 262144


def plant(values, own_key, low, largest):
    index_at = [jax.random.randint(jax.random.fold_in(own_key, axis), (), 0, length) for axis, length in enumerate(values.shape)]
    widest = values.shape.index(max(values.shape))
    neighbour = index_at[:widest] + [(index_at[widest] + 1) % values.shape[widest]] + index_at[widest + 1:]
    return values.at[tuple(index_at)].set(low).at[tuple(neighbour)].set(largest)


def shard_levels(stream_key, dims, split, smallest, top_value):
    def one(axis_at, parts):
        steps = jax.random.uniform(jax.random.fold_in(jax.random.fold_in(stream_key, 6), axis_at), (parts,), jnp.float32, smallest / len(split), top_value / len(split))
        return jnp.repeat(jnp.exp(steps), dims[axis_at] // parts).reshape((-1,) + (1,) * (len(dims) - axis_at - 1))

    loudness = one(*split[0])
    for cut in split[1:]:
        loudness = loudness * one(*cut)
    return loudness


def shared_out(key, own, number, rows, count, top, limit, slope):
    ranking = jax.random.permutation(key, count)
    packed, common = shares(count, rows * top, limit, slope, True), shares(count, rows * top, limit, slope, False)
    places = jnp.arange(count)

    def named(sizes, rotation):
        used = int((sizes > 0).sum())
        fixed = max(1, used // 4)
        moved = fixed + (places - fixed + rotation * (used - fixed)) % max(1, count - fixed)
        return jnp.zeros((count,), jnp.int32).at[ranking[jnp.where(places < fixed, places, moved)]].set(jnp.asarray(sizes, jnp.int32))

    sizes = jnp.where(number % 4 == 0, named(packed, number // 4), named(common, number - number // 4 - 1))
    mixed = jax.random.permutation(jax.random.fold_in(own, 3), count)
    source_of, receiver = mixed[0:count // 2 * 2:2], mixed[1:count // 2 * 2:2]
    margin = jnp.minimum(sizes[source_of] - 1, limit - sizes[receiver]) // 2
    margin = jnp.where((source_of == ranking[0]) | (receiver == ranking[0]) | (sizes[receiver] == 0), 0, jnp.maximum(margin, 0))
    moved = jax.random.randint(jax.random.fold_in(own, 4), (count // 2,), 0, 1 << 20) % (margin + 1)
    sizes = sizes.at[source_of].add(-moved).at[receiver].add(moved)
    members = jnp.searchsorted(jnp.cumsum(sizes), jnp.arange(rows * top), side="right").astype(jnp.int32)
    listing = members.reshape(top, rows).T
    listing = listing[jax.random.permutation(jax.random.fold_in(own, 1), rows)]
    rotation = jax.random.randint(jax.random.fold_in(own, 2), (rows, 1), 0, top)
    return jnp.take_along_axis(listing, (jnp.arange(top)[None, :] + rotation) % top, axis=1)


def shares(amount, total, limit, skew, full):
    weights = [(1 << 20) // math.isqrt(standing ** skew) + 1 for standing in range(1, amount + 1)]
    largest = limit if full else min(limit, max(-(-total // amount), total * weights[0] // sum(weights)))
    least = 1 if total - largest >= amount - 1 else 0
    given, surplus = [largest] + [least] * (amount - 1), total - largest - least * (amount - 1)
    while surplus > 0:
        free = [i for i in range(1, amount) if given[i] < largest] or [i for i in range(1, amount) if given[i] < limit]
        whole, budget = sum([weights[i] for i in free]), surplus
        for i in free:
            more = min(limit - given[i], max(1, budget * weights[i] // whole), surplus)
            given[i] = given[i] + more
            surplus = surplus - more
    return np.array(given)


def setup_inputs(seed: int = 0) -> dict:
    seeds = jax.random.split(jax.random.key(seed), 13)
    conc = jnp.clip(jnp.exp(math.log(10.0) - 4.6051702 * jax.random.uniform(seeds[0], (NC, LAYERS, COLUMNS), jnp.float32) ** shard_levels(seeds[0], (NC, LAYERS, COLUMNS), ((1, 32), (2, 16)), -0.2, 0.2)), 0.1, 10.0)
    porosity = jnp.clip(0.2 + 0.3 * jax.random.uniform(seeds[1], (LAYERS, COLUMNS), jnp.float32) ** shard_levels(seeds[1], (LAYERS, COLUMNS), ((0, 32), (1, 16)), -0.2, 0.2), 0.2, 0.5)
    cell_cond = jnp.clip(jnp.exp(math.log(2.0) - 1.3862944 * jax.random.uniform(seeds[2], (LAYERS, COLUMNS), jnp.float32) ** shard_levels(seeds[2], (LAYERS, COLUMNS), ((0, 32), (1, 16)), -0.2, 0.2)), 0.5, 2.0)
    soil_class = plant(jax.random.randint(seeds[3], (COLUMNS,), 0, NCLASS), jax.random.fold_in(seeds[3], 1), 0, NCLASS - 1).astype(jnp.int32)
    active = plant(jax.random.randint(seeds[4], (COLUMNS,), LAYERS // 4, LAYERS + 1), jax.random.fold_in(seeds[4], 1), LAYERS // 4, LAYERS).astype(jnp.int32)
    class_cond = jnp.clip(jnp.exp(jax.random.uniform(seeds[5], (NCLASS,), jnp.float32, math.log(20.0), math.log(400.0))), 20.0, 400.0)
    sorb_affinity = jnp.clip(jnp.exp(jax.random.uniform(seeds[6], (NCLASS, NC), jnp.float32, math.log(0.05), math.log(5.0))), 0.05, 5.0)
    sorb_capacity = jnp.clip(jnp.exp(jax.random.uniform(seeds[7], (NCLASS,), jnp.float32, math.log(1.0), math.log(20.0))), 1.0, 20.0)
    surf_conc = jnp.clip(jnp.exp(math.log(10.0) - 4.6051702 * jax.random.uniform(seeds[8], (NC, SURF), jnp.float32) ** shard_levels(seeds[8], (NC, SURF), ((1, 512),), -0.2, 0.2)), 0.1, 10.0)
    surf_rate = jnp.clip(jnp.exp(math.log(2.0) - 2.9957323 * jax.random.uniform(seeds[9], (SURF,), jnp.float32) ** shard_levels(seeds[9], (SURF,), ((0, 512),), -0.2, 0.2)), 0.1, 2.0)
    surf_group_keys = jax.random.split(jax.random.fold_in(seeds[10], 1), SURF // SURF_DEV)
    surf_group_turns = jax.random.permutation(jax.random.fold_in(seeds[10], 3), SURF // SURF_DEV)
    surf_group = jax.vmap(lambda own, number: shared_out(jax.random.fold_in(seeds[10], 2), own, number, SURF_DEV, GROUPS, 1, CAP, 2))(surf_group_keys, surf_group_turns).reshape((SURF, 1))
    surf_local = plant(jax.random.randint(seeds[11], (SURF,), 0, COL_DEV), jax.random.fold_in(seeds[11], 1), 0, COL_DEV - 1).astype(jnp.int32)
    return {"conc": conc, "porosity": porosity, "cell_cond": cell_cond, "soil_class": soil_class, "active": active, "class_cond": class_cond, "sorb_affinity": sorb_affinity, "sorb_capacity": sorb_capacity, "surf_conc": surf_conc, "surf_rate": surf_rate, "surf_group": surf_group, "surf_local": surf_local}


def interfaces(cell_values, class_scale, active_rows):
    scaled = cell_values * class_scale[None, :]
    upper_cell = scaled[:-1]
    lower_cell = scaled[1:]
    harmonic = 2.0 * upper_cell * lower_cell / (upper_cell + lower_cell)
    depth_ids = lax.broadcasted_iota(jnp.int32, harmonic.shape, 0)
    return jnp.where(depth_ids + 1 < active_rows[None, :], harmonic, jnp.zeros_like(harmonic))

def vertical_solve(totals_old, theta, couplings, source, sink):
    zero_row = jnp.zeros_like(couplings[:1])
    link_above = jnp.concatenate([zero_row, couplings], axis=0)
    link_below = jnp.concatenate([couplings, zero_row], axis=0)
    is_top = lax.broadcasted_iota(jnp.int32, theta.shape, 0) == 0
    diagonal = theta + link_above + link_below + jnp.where(is_top, sink[None, :], jnp.zeros_like(theta))
    right_side = theta[None] * totals_old + jnp.where(is_top[None], source[:, None, :], jnp.zeros_like(totals_old))
    solved = lax.linalg.tridiagonal_solve((-link_above).T, diagonal.T, (-link_below).T, jnp.transpose(right_side, (2, 1, 0)))
    return jnp.transpose(solved, (2, 1, 0))

def speciate(totals, theta, affinity, capacity):
    sorbing = capacity[None, :] * affinity
    log_conc = jnp.log(totals / (theta[None] + sorbing[:, None, :]))
    for newton_step in range(ITERS):
        free_conc = jnp.exp(log_conc)
        crowding = 1.0 + jnp.sum(affinity[:, None, :] * free_conc, axis=0)
        slopes = theta[None] + sorbing[:, None, :] / crowding[None]
        misfit = free_conc * slopes - totals
        coupling = sorbing[:, None, :] * free_conc / (crowding * crowding)[None]
        scaled_misfit = misfit / slopes
        leaning = coupling / slopes
        numerator = jnp.sum(affinity[:, None, :] * scaled_misfit, axis=0)
        denominator = 1.0 - jnp.sum(affinity[:, None, :] * leaning, axis=0)
        change = scaled_misfit + leaning * (numerator / denominator)[None]
        log_conc = log_conc - jnp.clip(change / free_conc, -1.0, 1.0)
    return log_conc

def reference(conc, porosity, cell_cond, soil_class, active, class_cond, sorb_affinity, sorb_capacity, surf_conc, surf_rate, surf_group, surf_local):
    row_ids = jnp.arange(SURF, dtype=jnp.int32)
    owner_col = surf_group[:, 0] * GC + row_ids // SURF_DEV % (GC // COL_DEV) * COL_DEV + surf_local
    weighted = surf_rate[None, :] * surf_conc
    source = jax.ops.segment_sum(weighted.T, owner_col, num_segments=COLUMNS).T
    sink = jax.ops.segment_sum(surf_rate, owner_col, num_segments=COLUMNS)
    class_scale = class_cond[soil_class]
    capacity = sorb_capacity[soil_class]
    affinity = sorb_affinity[soil_class].T
    block_count = COLUMNS // COL_DEV

    def one_block(block_id):
        first_col = block_id * COL_DEV

        def window(array):
            return lax.dynamic_slice_in_dim(array, first_col, COL_DEV, array.ndim - 1)
        couplings = interfaces(window(cell_cond), window(class_scale), window(active))
        totals = vertical_solve(window(conc), window(porosity), couplings, window(source), window(sink))
        return (totals[:, 0, :], speciate(totals, window(porosity), window(affinity), window(capacity)))
    top_layers, log_blocks = lax.map(one_block, jnp.arange(block_count, dtype=jnp.int32))
    top_all = jnp.transpose(top_layers, (1, 0, 2)).reshape(NC, COLUMNS)
    log_free = jnp.transpose(log_blocks, (1, 2, 0, 3)).reshape(NC, LAYERS, COLUMNS)
    surf_flux = weighted - surf_rate[None, :] * jnp.take(top_all, owner_col, axis=1)
    return (log_free, surf_flux)
```

```python
import functools
import jax
import jax.numpy as jnp
from jax import lax
from jax.experimental import pallas as pl
from jax.experimental.pallas import tpu as pltpu
from jax.sharding import PartitionSpec as P

ITERS = 4
LANES = 128
F32 = jnp.float32
INTERPRET = False


def split3(v):
    hi = v.astype(jnp.bfloat16)
    rest = v - hi.astype(F32)
    mid = rest.astype(jnp.bfloat16)
    lo = (rest - mid.astype(F32)).astype(jnp.bfloat16)
    return hi, mid, lo


def rows_iota(shape):
    return lax.broadcasted_iota(jnp.int32, shape, 0)


def surf_pack_kernel(conc_ref, rate_ref, group_ref, local_ref, send_ref, lhs_ref):
    comps, n = conc_ref.shape
    groups = send_ref.shape[0]
    rate = rate_ref[...]
    vals = jnp.concatenate(
        [conc_ref[...] * rate, rate, jnp.zeros((15 - comps, n), F32)], axis=0
    )
    hi, mid, lo = split3(vals)
    group = group_ref[...]
    for g in range(groups):
        keep = group == g
        for i, part in enumerate((hi, mid, lo)):
            lhs_ref[i, 16 * g : 16 * g + 16, :] = jnp.where(
                keep, part.astype(F32), 0.0
            ).astype(jnp.bfloat16)
    place = (rows_iota((LANES, n)) == local_ref[...]).astype(F32).astype(jnp.bfloat16)
    dims = (((1,), (1,)), ((), ()))
    total = sum(
        lax.dot_general(lhs_ref[i], place, dims, preferred_element_type=F32)
        for i in (2, 1, 0)
    )
    send_ref[...] = total.reshape(groups, 16, LANES)


def surf_flux_kernel(table_ref, conc_ref, rate_ref, group_ref, local_ref, flux_ref):
    comps, n = conc_ref.shape
    groups = table_ref.shape[0]
    table = table_ref[...].reshape(groups * 16, LANES)
    place = (rows_iota((LANES, n)) == local_ref[...]).astype(F32).astype(jnp.bfloat16)
    hi, mid, lo = split3(table)
    picked = jnp.dot(lo, place, preferred_element_type=F32)
    picked += jnp.dot(mid, place, preferred_element_type=F32)
    picked += jnp.dot(hi, place, preferred_element_type=F32)
    group = group_ref[...]
    top = jnp.zeros((16, n), F32)
    for g in range(groups):
        top = jnp.where(group == g, picked[16 * g : 16 * g + 16], top)
    rate = rate_ref[...]
    flux_ref[...] = rate * conc_ref[...] - rate * top[:comps]


def eliminate_kernel(
    first_ref, table_ref, conc_ref, theta_ref, cond_ref, meta_ref, send_ref, g_ref, vw_ref
):
    comps = conc_ref.shape[0]
    tiles = send_ref.shape[0]
    shape = (8, LANES)
    row = rows_iota(shape)
    zero = jnp.zeros(shape, F32)
    layer = first_ref[0] + row

    def roll(v, d):
        return pltpu.roll(v, d % 8, 0)

    for t in range(tiles):
        cols = pl.ds(t * LANES, LANES)
        classes = meta_ref[t, 0:1, :]
        active = meta_ref[t, 1:2, :]
        scale = jnp.zeros((1, LANES), F32)
        for k in range(table_ref.shape[0]):
            scale = jnp.where(classes == k, table_ref[k], scale)
        theta = theta_ref[:, cols]
        scaled = cond_ref[:, cols] * scale
        below = roll(scaled, -1)
        link = 2.0 * scaled * below / (scaled + below)
        link = jnp.where((row < 7) & (layer + 1 < active), link, zero)
        link_up = roll(link, 1)
        up = jnp.where((row >= 2) & (row <= 6), link_up, zero)
        dn = jnp.where((row >= 1) & (row <= 5), link, zero)
        r_v = jnp.where(row == 1, link_up, zero)
        r_w = jnp.where(row == 6, link, zero)
        r_e = jnp.where((row >= 1) & (row <= 6), theta, zero)
        excess = theta + r_v + r_w
        w1 = 1.0 / (excess + up + dn)
        t1 = excess * w1
        up1, dn1 = up, dn
        excess = excess + up * roll(t1, 1) + dn * roll(t1, -1)
        up2 = up * roll(up * w1, 1)
        dn2 = dn * roll(dn * w1, -1)
        w2 = 1.0 / (excess + up2 + dn2)
        t2 = excess * w2
        excess = excess + up2 * roll(t2, 2) + dn2 * roll(t2, -2)
        up3 = up2 * roll(up2 * w2, 2)
        dn3 = dn2 * roll(dn2 * w2, -2)
        far = up3 + dn3
        w3 = 1.0 / (excess + far)
        excess = excess + far * roll(excess * w3, 4)
        w4 = 1.0 / excess

        def solve(r):
            q = r * w1
            r = r + up1 * roll(q, 1) + dn1 * roll(q, -1)
            q = r * w2
            r = r + up2 * roll(q, 2) + dn2 * roll(q, -2)
            r = r + far * roll(r * w3, 4)
            return r * w4

        ends = jnp.where(row == 0, link, zero) + jnp.where(row == 7, link_up, zero)

        def onto_ends(own, inner):
            near = jnp.where(row == 0, roll(inner, -1), roll(inner, 1))
            return own + ends * near

        v = solve(r_v)
        w = solve(r_w)
        e = solve(r_e)
        vw_ref[0, :, cols] = jnp.where(row == 0, 1.0, v)
        vw_ref[1, :, cols] = jnp.where(row == 7, 1.0, w)
        diag = onto_ends(theta, e)
        cross = onto_ends(zero, w)
        mat = jnp.where(row == 0, diag, zero)
        mat = jnp.where(row == 1, roll(diag, 2), mat)
        mat = jnp.where(row == 2, roll(cross, 2), mat)
        mat = jnp.where(row == 3, roll(scaled, 3), mat)
        mat = jnp.where(row == 4, roll(scaled, 5), mat)
        send_ref[t, 24:32, :] = mat
        firsts, lasts, mixed = zero, zero, zero
        for j in range(comps):
            c = conc_ref[j, :, cols]
            g = solve(r_e * c)
            g_ref[j, :, cols] = g
            z = onto_ends(theta * c, g)
            if j < 8:
                z = roll(z, j) if j else z
                firsts = jnp.where(row == j, z, firsts)
                lasts = jnp.where(row == (j + 7) % 8, z, lasts)
            else:
                k = j - 8
                mixed = jnp.where(row == k, roll(z, k) if k else z, mixed)
                mixed = jnp.where(row == k + 4, roll(z, k + 5), mixed)
        send_ref[t, 0:8, :] = firsts
        send_ref[t, 8:16, :] = lasts
        send_ref[t, 16:24, :] = mixed


def first_row(j):
    return j if j < 8 else 16 + j - 8


def last_row(j):
    return 8 + (j + 7) % 8 if j < 8 else 20 + j - 8


def interface_kernel(recv_ref, surf_ref, active_ref, ends_ref, top_ref):
    blocks = ends_ref.shape[0] // 24
    comps = 12
    groups = top_ref.shape[0]
    shape = (blocks, LANES)
    row = rows_iota(shape)
    zero = jnp.zeros(shape, F32)

    def roll(v, d):
        return pltpu.roll(v, d % blocks, 0)

    def take(r):
        return recv_ref[pl.ds(r, blocks, stride=32), :]

    partial = surf_ref[0]
    for g in range(1, surf_ref.shape[0]):
        partial = partial + surf_ref[g]
    alpha = take(24) + jnp.where(row == 0, partial[comps : comps + 1], zero)
    beta, cross, s_first, s_last = take(25), take(26), take(27), take(28)
    s_above = roll(s_last, 1)
    link = 2.0 * s_above * s_first / (s_above + s_first)
    link = jnp.where((row > 0) & (8 * row < active_ref[...]), link, zero)
    wf = 1.0 / (alpha + cross + link)
    cross_w = cross * wf
    link_w = link * wf
    up = link * cross_w
    dn = roll(up, -1)
    excess = beta + alpha * cross_w + roll(alpha * link_w, -1)
    steps = []
    d = 1
    while d < blocks:
        w = 1.0 / (excess + up + dn)
        steps.append((d, up, dn, w))
        q = excess * w
        excess = excess + up * roll(q, d) + dn * roll(q, -d)
        up, dn = up * roll(up * w, d), dn * roll(dn * w, -d)
        d *= 2
    w_end = 1.0 / excess
    tops = []
    for j in range(comps):
        b = take(first_row(j)) + jnp.where(row == 0, partial[j : j + 1], zero)
        r = take(last_row(j)) + cross_w * b + roll(link_w * b, -1)
        for d, up, dn, w in steps:
            q = r * w
            r = r + up * roll(q, d) + dn * roll(q, -d)
        last = r * w_end
        first = link_w * roll(last, 1) + cross_w * last + wf * b
        ends_ref[pl.ds(j, blocks, stride=24), :] = first
        ends_ref[pl.ds(12 + j, blocks, stride=24), :] = last
        tops.append(first[0:1])
    top = jnp.concatenate(tops + [jnp.zeros((16 - comps, LANES), F32)], axis=0)
    for g in range(groups):
        top_ref[g] = top


def lookup_kernel(table_ref, meta_ref, out_ref):
    table = table_ref[...]
    classes = table.shape[1]
    hi, mid, lo = split3(table)
    for t in range(out_ref.shape[0]):
        hit = (rows_iota((classes, LANES)) == meta_ref[t, 0:1, :]).astype(F32)
        hit = hit.astype(jnp.bfloat16)
        out_ref[t] = (
            jnp.dot(lo, hit, preferred_element_type=F32)
            + jnp.dot(mid, hit, preferred_element_type=F32)
            + jnp.dot(hi, hit, preferred_element_type=F32)
        )


def speciate_kernel(g_ref, vw_ref, theta_ref, ends_ref, sorb_ref, out_ref):
    comps = g_ref.shape[0]
    tiles = ends_ref.shape[0]

    def tile(t, carry):
        cols = pl.ds(pl.multiple_of(t * LANES, LANES), LANES)
        theta = theta_ref[:, cols]
        v = vw_ref[0, :, cols]
        w = vw_ref[1, :, cols]
        cap = sorb_ref[t, comps : comps + 1, :]
        aff = [sorb_ref[t, j : j + 1, :] for j in range(comps)]
        sorb = [cap * a for a in aff]
        x, c, p, at = [], [], [], []
        for j in range(comps):
            total = (
                g_ref[j, :, cols]
                + v * ends_ref[t, j : j + 1, :]
                + w * ends_ref[t, 12 + j : 13 + j, :]
            )
            whole = theta + sorb[j]
            start = total / whole
            x.append(jnp.log(start))
            c.append(start)
            p.append(whole)
            at.append(aff[j] * total)
        for step in range(ITERS):
            ac = [aff[j] * c[j] for j in range(comps)]
            load = sum(ac[1:], ac[0])
            crowd = 1.0 + load
            hold = theta * crowd
            q = [1.0 / (hold + sorb[j]) for j in range(comps)]
            sq = [sorb[j] * q[j] for j in range(comps)]
            atq = [at[j] * q[j] for j in range(comps)]
            acq = [ac[j] * sq[j] for j in range(comps)]
            numer = load - crowd * sum(atq[1:], atq[0])
            lean = sum(acq[1:], acq[0])
            gain = 1.0 + numer / (crowd - lean)
            for j in range(comps):
                move = (theta - p[j]) * crowd * q[j] + sq[j] * gain
                move = jnp.clip(move, -1.0, 1.0)
                x[j] = x[j] - move
                if step < ITERS - 1:
                    c[j] = c[j] * jnp.exp(-move)
                    p[j] = p[j] * jnp.exp(move)
        for j in range(comps):
            out_ref[j, :, cols] = x[j]
        return carry

    lax.fori_loop(0, tiles, tile, 0)


VMEM = pltpu.VMEM


def full(memory_space=VMEM):
    return pl.BlockSpec(memory_space=memory_space)


def call(kernel, out_shape, n_in, **kw):
    n_out = len(out_shape) if isinstance(out_shape, (tuple, list)) else None
    out_specs = full() if n_out is None else tuple(full() for _ in range(n_out))
    return pl.pallas_call(
        kernel,
        out_shape=out_shape,
        in_specs=[full()] * n_in,
        out_specs=out_specs,
        interpret=INTERPRET,
        **kw,
    )


def body(
    conc,
    porosity,
    cell_cond,
    soil_class,
    active,
    class_cond,
    sorb_affinity,
    sorb_capacity,
    surf_conc,
    surf_rate,
    surf_group,
    surf_local,
):
    groups = lax.axis_size("grp")
    owners = lax.axis_size("col")
    comps, depth, width = conc.shape
    n = surf_conc.shape[1]
    sds = jax.ShapeDtypeStruct
    first = (lax.axis_index("col") * depth).astype(jnp.int32).reshape(1)

    meta = jnp.stack([soil_class, active])
    meta = jnp.broadcast_to(meta[None], (owners, 2, LANES))
    meta = lax.all_to_all(meta, "col", split_axis=0, concat_axis=0, tiled=True)

    rate = surf_rate.reshape(1, n)
    group = surf_group.reshape(1, n)
    local = surf_local.reshape(1, n)
    surf_send = call(
        surf_pack_kernel,
        sds((groups, 16, LANES), F32),
        4,
        scratch_shapes=[pltpu.VMEM((3, 16 * groups, n), jnp.bfloat16)],
        name="surf_pack",
    )(surf_conc, rate, group, local)
    surf_recv = lax.all_to_all(surf_send, "grp", split_axis=0, concat_axis=0, tiled=True)

    tiles = 4
    steps = owners // tiles
    wide = tiles * LANES
    send, g, vw = pl.pallas_call(
        eliminate_kernel,
        grid=(steps,),
        out_shape=(
            sds((owners, 32, LANES), F32),
            sds((comps, depth, width), F32),
            sds((2, depth, width), F32),
        ),
        in_specs=[
            pl.BlockSpec(memory_space=pltpu.SMEM),
            pl.BlockSpec(memory_space=pltpu.SMEM),
            pl.BlockSpec((comps, depth, wide), lambda i: (0, 0, i)),
            pl.BlockSpec((depth, wide), lambda i: (0, i)),
            pl.BlockSpec((depth, wide), lambda i: (0, i)),
            pl.BlockSpec((tiles, 2, LANES), lambda i: (i, 0, 0)),
        ],
        out_specs=(
            pl.BlockSpec((tiles, 32, LANES), lambda i: (i, 0, 0)),
            pl.BlockSpec((comps, depth, wide), lambda i: (0, 0, i)),
            pl.BlockSpec((2, depth, wide), lambda i: (0, 0, i)),
        ),
        interpret=INTERPRET,
        name="eliminate",
    )(first, class_cond, conc, porosity, cell_cond, meta)
    recv = lax.all_to_all(send, "col", split_axis=0, concat_axis=0, tiled=True)

    table = jnp.concatenate(
        [sorb_affinity.T, sorb_capacity[None], jnp.zeros((15 - comps, 16), F32)], axis=0
    )
    sorb = call(lookup_kernel, sds((owners, 16, LANES), F32), 2, name="lookup")(table, meta)

    ends, top = call(
        interface_kernel,
        (sds((owners * 24, LANES), F32), sds((groups, 16, LANES), F32)),
        3,
        name="interface",
    )(recv.reshape(owners * 32, LANES), surf_recv, active.reshape(1, LANES))
    ends = lax.all_to_all(
        ends.reshape(owners, 24, LANES), "col", split_axis=0, concat_axis=0, tiled=True
    )
    top = lax.all_to_all(top, "grp", split_axis=0, concat_axis=0, tiled=True)

    log_free = pl.pallas_call(
        speciate_kernel,
        grid=(steps,),
        out_shape=sds((comps, depth, width), F32),
        in_specs=[
            pl.BlockSpec((comps, depth, wide), lambda i: (0, 0, i)),
            pl.BlockSpec((2, depth, wide), lambda i: (0, 0, i)),
            pl.BlockSpec((depth, wide), lambda i: (0, i)),
            pl.BlockSpec((tiles, 24, LANES), lambda i: (i, 0, 0)),
            pl.BlockSpec((tiles, 16, LANES), lambda i: (i, 0, 0)),
        ],
        out_specs=pl.BlockSpec((comps, depth, wide), lambda i: (0, 0, i)),
        interpret=INTERPRET,
        name="speciate",
    )(g, vw, porosity, ends, sorb)

    flux = call(surf_flux_kernel, sds((comps, n), F32), 5, name="surf_flux")(
        top, surf_conc, rate, group, local
    )
    return (log_free, flux)


def solution(mesh):
    return jax.shard_map(
        body,
        mesh=mesh,
        in_specs=(
            P(None, "col", "grp"),
            P("col", "grp"),
            P("col", "grp"),
            P(("grp", "col")),
            P(("grp", "col")),
            P(),
            P(),
            P(),
            P(None, ("grp", "col")),
            P(("grp", "col")),
            P(("grp", "col"), None),
            P(("grp", "col")),
        ),
        out_specs=(P(None, "col", "grp"), P(None, ("grp", "col"))),
        check_vma=False,
    )
```

```python
import jax
import jax.numpy as jnp
from jax import lax
from jax.experimental import pallas as pl
from jax.experimental.pallas import tpu as pltpu
from jax.sharding import PartitionSpec as P

ITERS = 4
LANES = 128
F32 = jnp.float32
INTERPRET = False


def split3(v):
    hi = v.astype(jnp.bfloat16)
    rest = v - hi.astype(F32)
    mid = rest.astype(jnp.bfloat16)
    lo = (rest - mid.astype(F32)).astype(jnp.bfloat16)
    return hi, mid, lo


def rows_iota(shape):
    return lax.broadcasted_iota(jnp.int32, shape, 0)


def surf_pack_kernel(conc_ref, rate_ref, group_ref, local_ref, send_ref, lhs_ref):
    comps, n = conc_ref.shape
    groups = send_ref.shape[0]
    rate = rate_ref[...]
    vals = jnp.concatenate(
        [conc_ref[...] * rate, rate, jnp.zeros((15 - comps, n), F32)], axis=0
    )
    hi, mid, lo = split3(vals)
    group = group_ref[...]
    for g in range(groups):
        keep = group == g
        for i, part in enumerate((hi, mid, lo)):
            lhs_ref[i, 16 * g : 16 * g + 16, :] = jnp.where(
                keep, part.astype(F32), 0.0
            ).astype(jnp.bfloat16)
    place = (rows_iota((LANES, n)) == local_ref[...]).astype(F32).astype(jnp.bfloat16)
    dims = (((1,), (1,)), ((), ()))
    total = sum(
        lax.dot_general(lhs_ref[i], place, dims, preferred_element_type=F32)
        for i in (2, 1, 0)
    )
    send_ref[...] = total.reshape(groups, 16, LANES)


def surf_flux_kernel(table_ref, conc_ref, rate_ref, group_ref, local_ref, flux_ref):
    comps, n = conc_ref.shape
    groups = table_ref.shape[0]
    table = table_ref[...].reshape(groups * 16, LANES)
    place = (rows_iota((LANES, n)) == local_ref[...]).astype(F32).astype(jnp.bfloat16)
    hi, mid, lo = split3(table)
    picked = jnp.dot(lo, place, preferred_element_type=F32)
    picked += jnp.dot(mid, place, preferred_element_type=F32)
    picked += jnp.dot(hi, place, preferred_element_type=F32)
    group = group_ref[...]
    top = jnp.zeros((16, n), F32)
    for g in range(groups):
        top = jnp.where(group == g, picked[16 * g : 16 * g + 16], top)
    rate = rate_ref[...]
    flux_ref[...] = rate * conc_ref[...] - rate * top[:comps]


def eliminate_kernel(
    first_ref,
    table_ref,
    conc_hbm,
    theta_hbm,
    cond_hbm,
    meta_ref,
    send_ref,
    g_ref,
    vw_ref,
    conc_ref,
    theta_ref,
    cond_ref,
    sems,
):
    comps = conc_ref.shape[0]
    wide = conc_ref.shape[2] // CHUNKS

    def in_copies(n):
        part = pl.ds(pl.multiple_of(n * wide, wide), wide)
        return [
            pltpu.make_async_copy(
                theta_hbm.at[:, part], theta_ref.at[:, part], sems.at[3 * n]
            ),
            pltpu.make_async_copy(
                cond_hbm.at[:, part], cond_ref.at[:, part], sems.at[3 * n + 1]
            ),
            pltpu.make_async_copy(
                conc_hbm.at[:, :, part], conc_ref.at[:, :, part], sems.at[3 * n + 2]
            ),
        ]

    for n in range(CHUNKS):
        for copy in in_copies(n):
            copy.start()
    tiles = send_ref.shape[0]
    shape = (8, LANES)
    row = rows_iota(shape)
    zero = jnp.zeros(shape, F32)
    layer = first_ref[0] + row

    def roll(v, d):
        return pltpu.roll(v, d % 8, 0)

    def tile(t):
        cols = pl.ds(pl.multiple_of(t * LANES, LANES), LANES)
        classes = meta_ref[t, 0:1, :]
        active = meta_ref[t, 1:2, :]
        scale = jnp.zeros((1, LANES), F32)
        for k in range(table_ref.shape[0]):
            scale = jnp.where(classes == k, table_ref[k], scale)
        theta = theta_ref[:, cols]
        scaled = cond_ref[:, cols] * scale
        below = roll(scaled, -1)
        link = 2.0 * scaled * below / (scaled + below)
        link = jnp.where((row < 7) & (layer + 1 < active), link, zero)
        link_up = roll(link, 1)
        up = jnp.where((row >= 2) & (row <= 6), link_up, zero)
        dn = jnp.where((row >= 1) & (row <= 5), link, zero)
        r_v = jnp.where(row == 1, link_up, zero)
        r_w = jnp.where(row == 6, link, zero)
        r_e = jnp.where((row >= 1) & (row <= 6), theta, zero)
        excess = theta + r_v + r_w
        w1 = 1.0 / (excess + up + dn)
        t1 = excess * w1
        up1, dn1 = up, dn
        excess = excess + up * roll(t1, 1) + dn * roll(t1, -1)
        up2 = up * roll(up * w1, 1)
        dn2 = dn * roll(dn * w1, -1)
        w2 = 1.0 / (excess + up2 + dn2)
        t2 = excess * w2
        excess = excess + up2 * roll(t2, 2) + dn2 * roll(t2, -2)
        up3 = up2 * roll(up2 * w2, 2)
        dn3 = dn2 * roll(dn2 * w2, -2)
        far = up3 + dn3
        w3 = 1.0 / (excess + far)
        excess = excess + far * roll(excess * w3, 4)
        w4 = 1.0 / excess

        def solve(r):
            q = r * w1
            r = r + up1 * roll(q, 1) + dn1 * roll(q, -1)
            q = r * w2
            r = r + up2 * roll(q, 2) + dn2 * roll(q, -2)
            r = r + far * roll(r * w3, 4)
            return r * w4

        ends = jnp.where(row == 0, link, zero) + jnp.where(row == 7, link_up, zero)

        def onto_ends(own, inner):
            near = jnp.where(row == 0, roll(inner, -1), roll(inner, 1))
            return own + ends * near

        v = solve(r_v)
        w = solve(r_w)
        e = solve(r_e)
        vw_ref[0, :, cols] = jnp.where(row == 0, 1.0, v)
        vw_ref[1, :, cols] = jnp.where(row == 7, 1.0, w)
        diag = onto_ends(theta, e)
        cross = onto_ends(zero, w)
        mat = jnp.where(row == 0, diag, zero)
        mat = jnp.where(row == 1, roll(diag, 2), mat)
        mat = jnp.where(row == 2, roll(cross, 2), mat)
        mat = jnp.where(row == 3, roll(scaled, 3), mat)
        mat = jnp.where(row == 4, roll(scaled, 5), mat)
        send_ref[t, 24:32, :] = mat
        firsts, lasts, mixed = zero, zero, zero
        for j in range(comps):
            c = conc_ref[j, :, cols]
            g = solve(r_e * c)
            g_ref[j, :, cols] = g
            z = onto_ends(theta * c, g)
            if j < 8:
                z = roll(z, j) if j else z
                firsts = jnp.where(row == j, z, firsts)
                lasts = jnp.where(row == (j + 7) % 8, z, lasts)
            else:
                k = j - 8
                mixed = jnp.where(row == k, roll(z, k) if k else z, mixed)
                mixed = jnp.where(row == k + 4, roll(z, k + 5), mixed)
        send_ref[t, 0:8, :] = firsts
        send_ref[t, 8:16, :] = lasts
        send_ref[t, 16:24, :] = mixed

    def tiles_of(i, carry):
        for k in range(FEW):
            tile(i * FEW + k)
        return carry

    per = tiles // FEW // CHUNKS

    def chunk(n, carry):
        for copy in in_copies(n):
            copy.wait()
        lax.fori_loop(n * per, (n + 1) * per, tiles_of, 0)
        return carry

    lax.fori_loop(0, CHUNKS, chunk, 0)


FEW = 4


def first_row(j):
    return j if j < 8 else 16 + j - 8


def last_row(j):
    return 8 + (j + 7) % 8 if j < 8 else 20 + j - 8


def interface_kernel(recv_ref, surf_ref, active_ref, ends_ref, top_ref):
    blocks = ends_ref.shape[0] // 24
    comps = 12
    groups = top_ref.shape[0]
    shape = (blocks, LANES)
    row = rows_iota(shape)
    zero = jnp.zeros(shape, F32)

    def roll(v, d):
        return pltpu.roll(v, d % blocks, 0)

    def take(r):
        return recv_ref[pl.ds(r, blocks, stride=32), :]

    partial = surf_ref[0]
    for g in range(1, surf_ref.shape[0]):
        partial = partial + surf_ref[g]
    alpha = take(24) + jnp.where(row == 0, partial[comps : comps + 1], zero)
    beta, cross, s_first, s_last = take(25), take(26), take(27), take(28)
    s_above = roll(s_last, 1)
    link = 2.0 * s_above * s_first / (s_above + s_first)
    link = jnp.where((row > 0) & (8 * row < active_ref[...]), link, zero)
    wf = 1.0 / (alpha + cross + link)
    cross_w = cross * wf
    link_w = link * wf
    up = link * cross_w
    dn = roll(up, -1)
    excess = beta + alpha * cross_w + roll(alpha * link_w, -1)
    steps = []
    d = 1
    while d < blocks:
        w = 1.0 / (excess + up + dn)
        steps.append((d, up, dn, w))
        q = excess * w
        excess = excess + up * roll(q, d) + dn * roll(q, -d)
        up, dn = up * roll(up * w, d), dn * roll(dn * w, -d)
        d *= 2
    w_end = 1.0 / excess
    tops = []
    for j in range(comps):
        b = take(first_row(j)) + jnp.where(row == 0, partial[j : j + 1], zero)
        r = take(last_row(j)) + cross_w * b + roll(link_w * b, -1)
        for d, up, dn, w in steps:
            q = r * w
            r = r + up * roll(q, d) + dn * roll(q, -d)
        last = r * w_end
        first = link_w * roll(last, 1) + cross_w * last + wf * b
        ends_ref[pl.ds(j, blocks, stride=24), :] = first
        ends_ref[pl.ds(12 + j, blocks, stride=24), :] = last
        tops.append(first[0:1])
    top = jnp.concatenate(tops + [jnp.zeros((16 - comps, LANES), F32)], axis=0)
    for g in range(groups):
        top_ref[g] = top


def lookup_kernel(table_ref, meta_ref, out_ref):
    table = table_ref[...]
    classes = table.shape[1]
    hi, mid, lo = split3(table)
    for t in range(out_ref.shape[0]):
        hit = (rows_iota((classes, LANES)) == meta_ref[t, 0:1, :]).astype(F32)
        hit = hit.astype(jnp.bfloat16)
        out_ref[t] = (
            jnp.dot(lo, hit, preferred_element_type=F32)
            + jnp.dot(mid, hit, preferred_element_type=F32)
            + jnp.dot(hi, hit, preferred_element_type=F32)
        )


LOG2E = 1.4426950408889634
LN2 = 0.6931471805599453


def tree_sum(terms):
    while len(terms) > 1:
        terms = [
            terms[i] + terms[i + 1] if i + 1 < len(terms) else terms[i]
            for i in range(0, len(terms), 2)
        ]
    return terms[0]


def speciate_kernel(
    g_ref, vw_ref, theta_ref, ends_ref, sorb_ref, log_ref, out_ref, sems
):
    comps = g_ref.shape[0]
    tiles = ends_ref.shape[0]
    each = range(comps)
    wide = tiles * LANES // CHUNKS

    def out_copy(n):
        part = pl.ds(pl.multiple_of(n * wide, wide), wide)
        return pltpu.make_async_copy(
            out_ref.at[:, :, part], log_ref.at[:, :, part], sems.at[n]
        )

    def tile(i, carry):
        group = [i * PAIR + k for k in range(PAIR)]
        cells = range(len(group))
        cols = [pl.ds(pl.multiple_of(t * LANES, LANES), LANES) for t in group]
        theta = [theta_ref[:, n] for n in cols]
        c = [[None] * comps for _ in cells]
        p = [[None] * comps for _ in cells]
        at = [[None] * comps for _ in cells]

        def aff(k, j):
            return sorb_ref[group[k], j : j + 1, :]

        cap = [sorb_ref[t, comps : comps + 1, :] for t in group]
        for j in each:
            for k in cells:
                total = (
                    g_ref[j, :, cols[k]]
                    + vw_ref[0, :, cols[k]] * ends_ref[group[k], j : j + 1, :]
                    + vw_ref[1, :, cols[k]] * ends_ref[group[k], 12 + j : 13 + j, :]
                )
                whole = theta[k] + cap[k] * aff(k, j)
                c[k][j] = total / whole
                p[k][j] = whole
                at[k][j] = aff(k, j) * total
        for step in range(ITERS):
            for k in cells:
                ac = [aff(k, j) * c[k][j] for j in each]
                load = tree_sum(ac)
                crowd = 1.0 + load
                hold = theta[k] * crowd
                q = [1.0 / (hold + cap[k] * aff(k, j)) for j in each]
                sum_c = tree_sum([ac[j] * q[j] for j in each])
                sum_t = tree_sum([at[k][j] * q[j] for j in each])
                lift = (load - crowd * sum_t) / (1.0 + hold * sum_c) * LOG2E
                crowd = crowd * LOG2E
                held = hold * lift
                lift = lift + LOG2E
                for j in each:
                    move = q[j] * (p[k][j] * crowd + held) - lift
                    move = jnp.clip(move, -LOG2E, LOG2E)
                    if step < ITERS - 1:
                        grow = jnp.exp2(move)
                        c[k][j] = c[k][j] * grow
                        p[k][j] = p[k][j] / grow
                    else:
                        out_ref[j, :, cols[k]] = jnp.log(c[k][j]) + move * LN2
        return carry

    per = tiles // PAIR // CHUNKS

    def chunk(n, carry):
        lax.fori_loop(n * per, (n + 1) * per, tile, 0)
        out_copy(n).start()
        return carry

    lax.fori_loop(0, CHUNKS, chunk, 0)
    for n in range(CHUNKS):
        out_copy(n).wait()


PAIR = 2
CHUNKS = 4


VMEM = pltpu.VMEM


def full(memory_space=VMEM):
    return pl.BlockSpec(memory_space=memory_space)


def near(x):
    return x if INTERPRET else pltpu.with_memory_space_constraint(x, VMEM)


def held(shape):
    return jax.ShapeDtypeStruct(shape, F32) if INTERPRET else VMEM(shape, F32)


def call(kernel, out_shape, n_in, **kw):
    n_out = len(out_shape) if isinstance(out_shape, (tuple, list)) else None
    out_specs = full() if n_out is None else tuple(full() for _ in range(n_out))
    inner = pl.pallas_call(
        kernel,
        out_shape=out_shape,
        in_specs=[full()] * n_in,
        out_specs=out_specs,
        interpret=INTERPRET,
        compiler_params=pltpu.CompilerParams(vmem_limit_bytes=24 << 20),
        **kw,
    )
    return lambda *args: inner(*(near(a) for a in args))


def exchange(x, axis):
    return lax.all_to_all(x, axis, split_axis=0, concat_axis=0, tiled=True)


def step(
    conc,
    porosity,
    cell_cond,
    soil_class,
    active,
    class_cond,
    sorb_affinity,
    sorb_capacity,
    surf_conc,
    surf_rate,
    surf_group,
    surf_local,
):
    groups = lax.axis_size("grp")
    owners = lax.axis_size("col")
    comps, depth, width = conc.shape
    n = surf_conc.shape[1]
    sds = jax.ShapeDtypeStruct
    first = (lax.axis_index("col") * depth).astype(jnp.int32).reshape(1)

    kind = lax.broadcasted_iota(jnp.int32, (owners, 2, LANES), 1)
    meta = jnp.where(kind == 0, soil_class[None, None], active[None, None])
    meta = exchange(meta, "col")

    rate = surf_rate.reshape(1, n)
    group = surf_group.reshape(1, n)
    local = surf_local.reshape(1, n)
    surf_send = call(
        surf_pack_kernel,
        held((groups, 16, LANES)),
        4,
        scratch_shapes=[pltpu.VMEM((3, 16 * groups, n), jnp.bfloat16)],
        name="surf_pack",
    )(surf_conc, rate, group, local)
    surf_recv = exchange(surf_send, "grp")

    smem = pl.BlockSpec(memory_space=pltpu.SMEM)
    send, g, vw = pl.pallas_call(
        eliminate_kernel,
        out_shape=(
            held((owners, 32, LANES)),
            held((comps, depth, width)),
            held((2, depth, width)),
        ),
        in_specs=[smem, smem] + [pl.BlockSpec(memory_space=pl.ANY)] * 3 + [full()],
        out_specs=(full(), full(), full()),
        scratch_shapes=[
            pltpu.VMEM((comps, depth, width), F32),
            pltpu.VMEM((depth, width), F32),
            pltpu.VMEM((depth, width), F32),
            pltpu.SemaphoreType.DMA((3 * CHUNKS,)),
        ],
        interpret=INTERPRET,
        compiler_params=pltpu.CompilerParams(vmem_limit_bytes=24 << 20),
        name="eliminate",
    )(first, class_cond, conc, porosity, cell_cond, near(meta))
    recv = exchange(send, "col")

    table = jnp.concatenate(
        [sorb_affinity.T, sorb_capacity[None], jnp.zeros((15 - comps, 16), F32)], axis=0
    )
    sorb = call(lookup_kernel, held((owners, 16, LANES)), 2, name="lookup")(table, meta)

    ends, top = call(
        interface_kernel,
        (held((owners * 24, LANES)), held((groups, 16, LANES))),
        3,
        name="interface",
    )(recv.reshape(owners * 32, LANES), surf_recv, active.reshape(1, LANES))
    ends = exchange(ends.reshape(owners, 24, LANES), "col")
    top = exchange(top, "grp")

    log_free = pl.pallas_call(
        speciate_kernel,
        out_shape=sds((comps, depth, width), F32),
        in_specs=[full()] * 5,
        out_specs=pl.BlockSpec(memory_space=pl.ANY),
        scratch_shapes=[
            pltpu.VMEM((comps, depth, width), F32),
            pltpu.SemaphoreType.DMA((CHUNKS,)),
        ],
        interpret=INTERPRET,
        compiler_params=pltpu.CompilerParams(vmem_limit_bytes=24 << 20),
        name="speciate",
    )(near(g), near(vw), near(porosity), near(ends), near(sorb))

    flux = call(surf_flux_kernel, sds((comps, n), F32), 5, name="surf_flux")(
        top, surf_conc, rate, group, local
    )
    return (log_free, flux)


def solution(mesh):
    return jax.shard_map(
        step,
        mesh=mesh,
        in_specs=(
            P(None, "col", "grp"),
            P("col", "grp"),
            P("col", "grp"),
            P(("grp", "col")),
            P(("grp", "col")),
            P(),
            P(),
            P(),
            P(None, ("grp", "col")),
            P(("grp", "col")),
            P(("grp", "col"), None),
            P(("grp", "col")),
        ),
        out_specs=(P(None, "col", "grp"), P(None, ("grp", "col"))),
        check_vma=False,
    )
```

```python
import jax
import jax.numpy as jnp
from jax import lax
from jax.experimental import pallas as pl
from jax.experimental.pallas import tpu as pltpu
from jax.sharding import PartitionSpec as P

ITERS = 4
LANES = 128
F32 = jnp.float32
INTERPRET = False


def split3(v):
    hi = v.astype(jnp.bfloat16)
    rest = v - hi.astype(F32)
    mid = rest.astype(jnp.bfloat16)
    lo = (rest - mid.astype(F32)).astype(jnp.bfloat16)
    return hi, mid, lo


def rows_iota(shape):
    return lax.broadcasted_iota(jnp.int32, shape, 0)


def surf_pack_kernel(
    me_ref, conc_ref, rate_ref, group_ref, local_ref, keep_ref, send_ref, lhs_ref
):
    comps, n = conc_ref.shape
    half = send_ref.shape[0]
    rate = rate_ref[...]
    vals = jnp.concatenate(
        [conc_ref[...] * rate, rate, jnp.zeros((15 - comps, n), F32)], axis=0
    )
    parts = [part.astype(F32) for part in split3(vals)]
    slot = group_ref[...] ^ me_ref[0]
    for b in range(2 * half):
        keep = slot == b
        for i, part in enumerate(parts):
            lhs_ref[i, 16 * b : 16 * b + 16, :] = jnp.where(keep, part, 0.0).astype(
                jnp.bfloat16
            )
    place = (rows_iota((LANES, n)) == local_ref[...]).astype(F32).astype(jnp.bfloat16)
    dims = (((1,), (1,)), ((), ()))
    total = sum(
        lax.dot_general(lhs_ref[i], place, dims, preferred_element_type=F32)
        for i in (2, 1, 0)
    )
    total = total.reshape(2 * half, 16, LANES)
    keep_ref[...] = total[:half]
    send_ref[...] = total[half:]


def surf_flux_kernel(
    me_ref, near_ref, far_ref, conc_ref, rate_ref, group_ref, local_ref, flux_ref
):
    comps, n = conc_ref.shape
    half = far_ref.shape[0]
    place = (rows_iota((LANES, n)) == local_ref[...]).astype(F32).astype(jnp.bfloat16)
    table = jnp.concatenate([near_ref[...], far_ref[...]], axis=0)
    hi, mid, lo = split3(table.reshape(2 * half * 16, LANES))
    picked = jnp.dot(lo, place, preferred_element_type=F32)
    picked += jnp.dot(mid, place, preferred_element_type=F32)
    picked += jnp.dot(hi, place, preferred_element_type=F32)
    slot = group_ref[...] ^ me_ref[0]
    top = jnp.zeros((16, n), F32)
    for i in range(2 * half):
        top = jnp.where(slot == slot_mask(i, 2 * half), picked[16 * i : 16 * i + 16], top)
    rate = rate_ref[...]
    flux_ref[...] = rate * conc_ref[...] - rate * top[:comps]


def halvings(n):
    masks = []
    while n > 1:
        n //= 2
        masks.append(n)
    return masks


def slot_mask(i, n):
    return sum(m for k, m in enumerate(halvings(n)) if i >> k & 1)


def eliminate_kernel(
    first_ref,
    table_ref,
    conc_hbm,
    theta_hbm,
    cond_hbm,
    meta_ref,
    send_ref,
    g_ref,
    vw_ref,
    conc_ref,
    theta_ref,
    cond_ref,
    sems,
):
    comps = conc_ref.shape[0]
    wide = conc_ref.shape[2] // CHUNKS

    def in_copies(n):
        part = pl.ds(pl.multiple_of(n * wide, wide), wide)
        return [
            pltpu.make_async_copy(
                theta_hbm.at[:, part], theta_ref.at[:, part], sems.at[3 * n]
            ),
            pltpu.make_async_copy(
                cond_hbm.at[:, part], cond_ref.at[:, part], sems.at[3 * n + 1]
            ),
            pltpu.make_async_copy(
                conc_hbm.at[:, :, part], conc_ref.at[:, :, part], sems.at[3 * n + 2]
            ),
        ]

    for n in range(CHUNKS):
        for copy in in_copies(n):
            copy.start()
    tiles = send_ref.shape[0]
    shape = (8, LANES)
    row = rows_iota(shape)
    zero = jnp.zeros(shape, F32)
    layer = first_ref[0] + row

    def roll(v, d):
        return pltpu.roll(v, d % 8, 0)

    def tile(t):
        cols = pl.ds(pl.multiple_of(t * LANES, LANES), LANES)
        classes = meta_ref[t, 0:1, :]
        active = meta_ref[t, 1:2, :]
        scale = jnp.zeros((1, LANES), F32)
        for k in range(table_ref.shape[0]):
            scale = jnp.where(classes == k, table_ref[k], scale)
        theta = theta_ref[:, cols]
        scaled = cond_ref[:, cols] * scale
        below = roll(scaled, -1)
        link = 2.0 * scaled * below / (scaled + below)
        link = jnp.where((row < 7) & (layer + 1 < active), link, zero)
        link_up = roll(link, 1)
        up = jnp.where((row >= 2) & (row <= 6), link_up, zero)
        dn = jnp.where((row >= 1) & (row <= 5), link, zero)
        r_v = jnp.where(row == 1, link_up, zero)
        r_w = jnp.where(row == 6, link, zero)
        r_e = jnp.where((row >= 1) & (row <= 6), theta, zero)
        excess = theta + r_v + r_w
        w1 = 1.0 / (excess + up + dn)
        t1 = excess * w1
        up1, dn1 = up, dn
        excess = excess + up * roll(t1, 1) + dn * roll(t1, -1)
        up2 = up * roll(up * w1, 1)
        dn2 = dn * roll(dn * w1, -1)
        w2 = 1.0 / (excess + up2 + dn2)
        t2 = excess * w2
        excess = excess + up2 * roll(t2, 2) + dn2 * roll(t2, -2)
        up3 = up2 * roll(up2 * w2, 2)
        dn3 = dn2 * roll(dn2 * w2, -2)
        far = up3 + dn3
        w3 = 1.0 / (excess + far)
        excess = excess + far * roll(excess * w3, 4)
        w4 = 1.0 / excess

        def solve(r):
            q = r * w1
            r = r + up1 * roll(q, 1) + dn1 * roll(q, -1)
            q = r * w2
            r = r + up2 * roll(q, 2) + dn2 * roll(q, -2)
            r = r + far * roll(r * w3, 4)
            return r * w4

        ends = jnp.where(row == 0, link, zero) + jnp.where(row == 7, link_up, zero)

        def onto_ends(own, inner):
            near = jnp.where(row == 0, roll(inner, -1), roll(inner, 1))
            return own + ends * near

        v = solve(r_v)
        w = solve(r_w)
        e = solve(r_e)
        vw_ref[0, :, cols] = jnp.where(row == 0, 1.0, v)
        vw_ref[1, :, cols] = jnp.where(row == 7, 1.0, w)
        diag = onto_ends(theta, e)
        cross = onto_ends(zero, w)
        mat = jnp.where(row == 0, diag, zero)
        mat = jnp.where(row == 1, roll(diag, 2), mat)
        mat = jnp.where(row == 2, roll(cross, 2), mat)
        mat = jnp.where(row == 3, roll(scaled, 3), mat)
        mat = jnp.where(row == 4, roll(scaled, 5), mat)
        send_ref[t, 24:32, :] = mat
        firsts, lasts, mixed = zero, zero, zero
        for j in range(comps):
            c = conc_ref[j, :, cols]
            g = solve(r_e * c)
            g_ref[j, :, cols] = g
            z = onto_ends(theta * c, g)
            if j < 8:
                z = roll(z, j) if j else z
                firsts = jnp.where(row == j, z, firsts)
                lasts = jnp.where(row == (j + 7) % 8, z, lasts)
            else:
                k = j - 8
                mixed = jnp.where(row == k, roll(z, k) if k else z, mixed)
                mixed = jnp.where(row == k + 4, roll(z, k + 5), mixed)
        send_ref[t, 0:8, :] = firsts
        send_ref[t, 8:16, :] = lasts
        send_ref[t, 16:24, :] = mixed

    def tiles_of(i, carry):
        for k in range(FEW):
            tile(i * FEW + k)
        return carry

    per = tiles // FEW // CHUNKS

    def chunk(n, carry):
        for copy in in_copies(n):
            copy.wait()
        lax.fori_loop(n * per, (n + 1) * per, tiles_of, 0)
        return carry

    lax.fori_loop(0, CHUNKS, chunk, 0)


FEW = 4


def first_row(j):
    return j if j < 8 else 16 + j - 8


def last_row(j):
    return 8 + (j + 7) % 8 if j < 8 else 20 + j - 8


def interface_kernel(recv_ref, active_ref, *refs):
    *surf_refs, ends_ref, top_ref = refs
    blocks = ends_ref.shape[0] // 24
    comps = 12
    shape = (blocks, LANES)
    row = rows_iota(shape)
    zero = jnp.zeros(shape, F32)

    def roll(v, d):
        return pltpu.roll(v, d % blocks, 0)

    def take(r):
        return recv_ref[pl.ds(r, blocks, stride=32), :]

    partial = tree_sum([ref[0] for ref in surf_refs])
    alpha = take(24) + jnp.where(row == 0, partial[comps : comps + 1], zero)
    beta, cross, s_first, s_last = take(25), take(26), take(27), take(28)
    s_above = roll(s_last, 1)
    link = 2.0 * s_above * s_first / (s_above + s_first)
    link = jnp.where((row > 0) & (8 * row < active_ref[...]), link, zero)
    wf = 1.0 / (alpha + cross + link)
    cross_w = cross * wf
    link_w = link * wf
    up = link * cross_w
    dn = roll(up, -1)
    excess = beta + alpha * cross_w + roll(alpha * link_w, -1)
    steps = []
    d = 1
    while d < blocks:
        w = 1.0 / (excess + up + dn)
        steps.append((d, up, dn, w))
        q = excess * w
        excess = excess + up * roll(q, d) + dn * roll(q, -d)
        up, dn = up * roll(up * w, d), dn * roll(dn * w, -d)
        d *= 2
    w_end = 1.0 / excess
    tops = []
    for j in range(comps):
        b = take(first_row(j)) + jnp.where(row == 0, partial[j : j + 1], zero)
        r = take(last_row(j)) + cross_w * b + roll(link_w * b, -1)
        for d, up, dn, w in steps:
            q = r * w
            r = r + up * roll(q, d) + dn * roll(q, -d)
        last = r * w_end
        first = link_w * roll(last, 1) + cross_w * last + wf * b
        ends_ref[pl.ds(j, blocks, stride=24), :] = first
        ends_ref[pl.ds(12 + j, blocks, stride=24), :] = last
        tops.append(first[0:1])
    top_ref[0] = jnp.concatenate(
        tops + [jnp.zeros((16 - comps, LANES), F32)], axis=0
    )


def lookup_kernel(table_ref, meta_ref, out_ref):
    table = table_ref[...]
    classes = table.shape[1]
    hi, mid, lo = split3(table)
    for t in range(out_ref.shape[0]):
        hit = (rows_iota((classes, LANES)) == meta_ref[t, 0:1, :]).astype(F32)
        hit = hit.astype(jnp.bfloat16)
        out_ref[t] = (
            jnp.dot(lo, hit, preferred_element_type=F32)
            + jnp.dot(mid, hit, preferred_element_type=F32)
            + jnp.dot(hi, hit, preferred_element_type=F32)
        )


LOG2E = 1.4426950408889634
LN2 = 0.6931471805599453


def tree_sum(terms):
    while len(terms) > 1:
        terms = [
            terms[i] + terms[i + 1] if i + 1 < len(terms) else terms[i]
            for i in range(0, len(terms), 2)
        ]
    return terms[0]


def speciate_kernel(
    g_ref, vw_ref, theta_ref, ends_ref, sorb_ref, log_ref, out_ref, sems
):
    comps = g_ref.shape[0]
    tiles = ends_ref.shape[0]
    each = range(comps)
    wide = tiles * LANES // CHUNKS

    def out_copy(n):
        part = pl.ds(pl.multiple_of(n * wide, wide), wide)
        return pltpu.make_async_copy(
            out_ref.at[:, :, part], log_ref.at[:, :, part], sems.at[n]
        )

    def tile(i, carry):
        group = [i * PAIR + k for k in range(PAIR)]
        cells = range(len(group))
        cols = [pl.ds(pl.multiple_of(t * LANES, LANES), LANES) for t in group]
        theta = [theta_ref[:, n] for n in cols]
        c = [[None] * comps for _ in cells]
        p = [[None] * comps for _ in cells]
        at = [[None] * comps for _ in cells]

        def aff(k, j):
            return sorb_ref[group[k], j : j + 1, :]

        cap = [sorb_ref[t, comps : comps + 1, :] for t in group]
        for j in each:
            for k in cells:
                total = (
                    g_ref[j, :, cols[k]]
                    + vw_ref[0, :, cols[k]] * ends_ref[group[k], j : j + 1, :]
                    + vw_ref[1, :, cols[k]] * ends_ref[group[k], 12 + j : 13 + j, :]
                )
                whole = theta[k] + cap[k] * aff(k, j)
                c[k][j] = total / whole
                p[k][j] = whole
                at[k][j] = aff(k, j) * total
        for step in range(ITERS):
            for k in cells:
                ac = [aff(k, j) * c[k][j] for j in each]
                load = tree_sum(ac)
                crowd = 1.0 + load
                hold = theta[k] * crowd
                q = [1.0 / (hold + cap[k] * aff(k, j)) for j in each]
                sum_c = tree_sum([ac[j] * q[j] for j in each])
                sum_t = tree_sum([at[k][j] * q[j] for j in each])
                lift = (load - crowd * sum_t) / (1.0 + hold * sum_c) * LOG2E
                crowd = crowd * LOG2E
                held = hold * lift
                lift = lift + LOG2E
                for j in each:
                    move = q[j] * (p[k][j] * crowd + held) - lift
                    move = jnp.clip(move, -LOG2E, LOG2E)
                    if step < ITERS - 1:
                        grow = jnp.exp2(move)
                        c[k][j] = c[k][j] * grow
                        p[k][j] = p[k][j] / grow
                    else:
                        out_ref[j, :, cols[k]] = jnp.log(c[k][j]) + move * LN2
        return carry

    per = tiles // PAIR // CHUNKS

    def chunk(n, carry):
        lax.fori_loop(n * per, (n + 1) * per, tile, 0)
        out_copy(n).start()
        return carry

    lax.fori_loop(0, CHUNKS, chunk, 0)
    for n in range(CHUNKS):
        out_copy(n).wait()


PAIR = 2
CHUNKS = 4


VMEM, HBM = pltpu.VMEM, pltpu.HBM


def full(memory_space=VMEM):
    return pl.BlockSpec(memory_space=memory_space)


def near(x):
    return x if INTERPRET else pltpu.with_memory_space_constraint(x, VMEM)


def far(x):
    return x if INTERPRET else pltpu.with_memory_space_constraint(x, HBM)


def held(shape):
    return jax.ShapeDtypeStruct(shape, F32) if INTERPRET else VMEM(shape, F32)


def swap(x, mask):
    n = lax.axis_size("grp")
    return lax.ppermute(x, "grp", [(i, i ^ mask) for i in range(n)])


def call(kernel, out_shape, n_in, **kw):
    n_out = len(out_shape) if isinstance(out_shape, (tuple, list)) else None
    out_specs = full() if n_out is None else tuple(full() for _ in range(n_out))
    inner = pl.pallas_call(
        kernel,
        out_shape=out_shape,
        in_specs=[full()] * n_in,
        out_specs=out_specs,
        interpret=INTERPRET,
        compiler_params=pltpu.CompilerParams(vmem_limit_bytes=24 << 20),
        **kw,
    )
    return lambda *args: inner(*(near(a) for a in args))


def exchange(x, axis):
    return lax.all_to_all(x, axis, split_axis=0, concat_axis=0, tiled=True)


def step(
    conc,
    porosity,
    cell_cond,
    soil_class,
    active,
    class_cond,
    sorb_affinity,
    sorb_capacity,
    surf_conc,
    surf_rate,
    surf_group,
    surf_local,
):
    groups = lax.axis_size("grp")
    owners = lax.axis_size("col")
    comps, depth, width = conc.shape
    n = surf_conc.shape[1]
    sds = jax.ShapeDtypeStruct
    first = (lax.axis_index("col") * depth).astype(jnp.int32).reshape(1)

    kind = lax.broadcasted_iota(jnp.int32, (owners, 2, LANES), 1)
    meta = jnp.where(kind == 0, soil_class[None, None], active[None, None])
    meta = exchange(meta, "col")

    rate = surf_rate.reshape(1, n)
    group = surf_group.reshape(1, n)
    local = surf_local.reshape(1, n)
    smem = pl.BlockSpec(memory_space=pltpu.SMEM)
    me = lax.axis_index("grp").astype(jnp.int32).reshape(1)
    masks = halvings(groups)
    keep, surf_send = pl.pallas_call(
        surf_pack_kernel,
        out_shape=(
            sds((groups // 2, 16, LANES), F32),
            sds((groups // 2, 16, LANES), F32),
        ),
        in_specs=[smem] + [full()] * 4,
        out_specs=(full(), full()),
        scratch_shapes=[pltpu.VMEM((3, 16 * groups, n), jnp.bfloat16)],
        interpret=INTERPRET,
        compiler_params=pltpu.CompilerParams(vmem_limit_bytes=24 << 20),
        name="surf_pack",
    )(me, *(far(x) for x in (surf_conc, rate, group, local)))
    surf_parts = [keep]
    for k, mask in enumerate(masks):
        if k:
            surf_send = sum(x[mask : 2 * mask] for x in surf_parts)
        surf_parts.append(swap(surf_send, mask))
    surf_parts = [x[:1] for x in surf_parts]

    send, g, vw = pl.pallas_call(
        eliminate_kernel,
        out_shape=(
            held((owners, 32, LANES)),
            held((comps, depth, width)),
            held((2, depth, width)),
        ),
        in_specs=[smem, smem] + [pl.BlockSpec(memory_space=HBM)] * 3 + [full()],
        out_specs=(full(), full(), full()),
        scratch_shapes=[
            pltpu.VMEM((comps, depth, width), F32),
            pltpu.VMEM((depth, width), F32),
            pltpu.VMEM((depth, width), F32),
            pltpu.SemaphoreType.DMA((3 * CHUNKS,)),
        ],
        interpret=INTERPRET,
        compiler_params=pltpu.CompilerParams(vmem_limit_bytes=24 << 20),
        name="eliminate",
    )(first, far(class_cond), far(conc), far(porosity), far(cell_cond), near(meta))
    recv = exchange(send, "col")

    table = jnp.concatenate(
        [sorb_affinity.T, sorb_capacity[None], jnp.zeros((15 - comps, 16), F32)], axis=0
    )
    sorb = call(lookup_kernel, held((owners, 16, LANES)), 2, name="lookup")(table, meta)

    ends, top = call(
        interface_kernel,
        (held((owners * 24, LANES)), held((1, 16, LANES))),
        2 + len(surf_parts),
        name="interface",
    )(recv.reshape(owners * 32, LANES), active.reshape(1, LANES), *surf_parts)
    ends = exchange(ends.reshape(owners, 24, LANES), "col")
    for k, mask in enumerate(masks):
        if k:
            top = jnp.concatenate([top, other], axis=0)
        other = swap(top, mask)

    log_free = pl.pallas_call(
        speciate_kernel,
        out_shape=sds((comps, depth, width), F32),
        in_specs=[full()] * 5,
        out_specs=pl.BlockSpec(memory_space=pl.ANY),
        scratch_shapes=[
            pltpu.VMEM((comps, depth, width), F32),
            pltpu.SemaphoreType.DMA((CHUNKS,)),
        ],
        interpret=INTERPRET,
        compiler_params=pltpu.CompilerParams(vmem_limit_bytes=24 << 20),
        name="speciate",
    )(near(g), near(vw), near(porosity), near(ends), near(sorb))

    flux = pl.pallas_call(
        surf_flux_kernel,
        out_shape=sds((comps, n), F32),
        in_specs=[smem] + [full()] * 6,
        out_specs=full(),
        interpret=INTERPRET,
        compiler_params=pltpu.CompilerParams(vmem_limit_bytes=24 << 20),
        name="surf_flux",
    )(me, near(top), near(other), *(near(x) for x in (surf_conc, rate, group, local)))
    return (log_free, flux)


def solution(mesh):
    return jax.shard_map(
        step,
        mesh=mesh,
        in_specs=(
            P(None, "col", "grp"),
            P("col", "grp"),
            P("col", "grp"),
            P(("grp", "col")),
            P(("grp", "col")),
            P(),
            P(),
            P(),
            P(None, ("grp", "col")),
            P(("grp", "col")),
            P(("grp", "col"), None),
            P(("grp", "col")),
        ),
        out_specs=(P(None, "col", "grp"), P(None, ("grp", "col"))),
        check_vma=False,
    )
```

```python
import jax
import jax.numpy as jnp
from jax import lax
from jax.experimental import pallas as pl
from jax.experimental.pallas import tpu as pltpu
from jax.sharding import PartitionSpec as P

ITERS = 4
LANES = 128
F32 = jnp.float32
INTERPRET = False


def split3(v):
    hi = v.astype(jnp.bfloat16)
    rest = v - hi.astype(F32)
    mid = rest.astype(jnp.bfloat16)
    lo = (rest - mid.astype(F32)).astype(jnp.bfloat16)
    return hi, mid, lo


def rows_iota(shape):
    return lax.broadcasted_iota(jnp.int32, shape, 0)


def meta_kernel(class_ref, active_ref, out_ref):
    both = jnp.concatenate([class_ref[...], active_ref[...]], axis=0)
    for t in range(out_ref.shape[0]):
        out_ref[t] = both


def surf_pack_kernel(
    me_ref, conc_ref, rate_ref, group_ref, local_ref, keep_ref, send_ref, lhs_ref
):
    comps, n = conc_ref.shape
    half = send_ref.shape[0]
    rate = rate_ref[...]
    vals = jnp.concatenate(
        [conc_ref[...] * rate, rate, jnp.zeros((15 - comps, n), F32)], axis=0
    )
    parts = [part.astype(F32) for part in split3(vals)]
    slot = group_ref[...] ^ me_ref[0]
    for b in range(2 * half):
        keep = slot == b
        for i, part in enumerate(parts):
            lhs_ref[i, 16 * b : 16 * b + 16, :] = jnp.where(keep, part, 0.0).astype(
                jnp.bfloat16
            )
    place = (rows_iota((LANES, n)) == local_ref[...]).astype(F32).astype(jnp.bfloat16)
    dims = (((1,), (1,)), ((), ()))
    total = sum(
        lax.dot_general(lhs_ref[i], place, dims, preferred_element_type=F32)
        for i in (2, 1, 0)
    )
    total = total.reshape(2 * half, 16, LANES)
    keep_ref[...] = total[:half]
    send_ref[...] = total[half:]


def surf_flux_kernel(
    me_ref, near_ref, far_ref, conc_ref, rate_ref, group_ref, local_ref, flux_ref
):
    comps, n = conc_ref.shape
    half = far_ref.shape[0]
    place = (rows_iota((LANES, n)) == local_ref[...]).astype(F32).astype(jnp.bfloat16)
    table = jnp.concatenate([near_ref[...], far_ref[...]], axis=0)
    hi, mid, lo = split3(table.reshape(2 * half * 16, LANES))
    picked = jnp.dot(lo, place, preferred_element_type=F32)
    picked += jnp.dot(mid, place, preferred_element_type=F32)
    picked += jnp.dot(hi, place, preferred_element_type=F32)
    slot = group_ref[...] ^ me_ref[0]
    top = jnp.zeros((16, n), F32)
    for i in range(2 * half):
        top = jnp.where(slot == slot_mask(i, 2 * half), picked[16 * i : 16 * i + 16], top)
    rate = rate_ref[...]
    flux_ref[...] = rate * conc_ref[...] - rate * top[:comps]


def halvings(n):
    masks = []
    while n > 1:
        n //= 2
        masks.append(n)
    return masks


def doublings(n):
    masks = halvings(n)
    return [masks[k] for k in (0, 3, 2, 1) if k < len(masks)]


def slot_mask(i, n):
    return sum(m for k, m in enumerate(doublings(n)) if i >> k & 1)


def eliminate_kernel(
    first_ref,
    table_ref,
    conc_hbm,
    theta_hbm,
    cond_hbm,
    meta_ref,
    send_ref,
    g_ref,
    vw_ref,
    conc_ref,
    theta_ref,
    cond_ref,
    sems,
):
    comps = conc_ref.shape[0]
    wide = conc_ref.shape[2] // CHUNKS

    def in_copies(n):
        part = pl.ds(pl.multiple_of(n * wide, wide), wide)
        return [
            pltpu.make_async_copy(
                theta_hbm.at[:, part], theta_ref.at[:, part], sems.at[3 * n]
            ),
            pltpu.make_async_copy(
                cond_hbm.at[:, part], cond_ref.at[:, part], sems.at[3 * n + 1]
            ),
            pltpu.make_async_copy(
                conc_hbm.at[:, :, part], conc_ref.at[:, :, part], sems.at[3 * n + 2]
            ),
        ]

    for n in range(CHUNKS):
        for copy in in_copies(n):
            copy.start()
    tiles = send_ref.shape[0]
    shape = (8, LANES)
    row = rows_iota(shape)
    zero = jnp.zeros(shape, F32)
    layer = first_ref[0] + row

    def roll(v, d):
        return pltpu.roll(v, d % 8, 0)

    def tile(t):
        cols = pl.ds(pl.multiple_of(t * LANES, LANES), LANES)
        classes = meta_ref[t, 0:1, :]
        active = meta_ref[t, 1:2, :]
        scale = jnp.zeros((1, LANES), F32)
        for k in range(table_ref.shape[0]):
            scale = jnp.where(classes == k, table_ref[k], scale)
        theta = theta_ref[:, cols]
        scaled = cond_ref[:, cols] * scale
        below = roll(scaled, -1)
        link = 2.0 * scaled * below / (scaled + below)
        link = jnp.where((row < 7) & (layer + 1 < active), link, zero)
        link_up = roll(link, 1)
        up = jnp.where((row >= 2) & (row <= 6), link_up, zero)
        dn = jnp.where((row >= 1) & (row <= 5), link, zero)
        r_v = jnp.where(row == 1, link_up, zero)
        r_w = jnp.where(row == 6, link, zero)
        r_e = jnp.where((row >= 1) & (row <= 6), theta, zero)
        excess = theta + r_v + r_w
        w1 = 1.0 / (excess + up + dn)
        t1 = excess * w1
        up1, dn1 = up, dn
        excess = excess + up * roll(t1, 1) + dn * roll(t1, -1)
        up2 = up * roll(up * w1, 1)
        dn2 = dn * roll(dn * w1, -1)
        w2 = 1.0 / (excess + up2 + dn2)
        t2 = excess * w2
        excess = excess + up2 * roll(t2, 2) + dn2 * roll(t2, -2)
        up3 = up2 * roll(up2 * w2, 2)
        dn3 = dn2 * roll(dn2 * w2, -2)
        far = up3 + dn3
        w3 = 1.0 / (excess + far)
        excess = excess + far * roll(excess * w3, 4)
        w4 = 1.0 / excess

        def solve(r):
            q = r * w1
            r = r + up1 * roll(q, 1) + dn1 * roll(q, -1)
            q = r * w2
            r = r + up2 * roll(q, 2) + dn2 * roll(q, -2)
            r = r + far * roll(r * w3, 4)
            return r * w4

        ends = jnp.where(row == 0, link, zero) + jnp.where(row == 7, link_up, zero)

        def onto_ends(own, inner):
            near = jnp.where(row == 0, roll(inner, -1), roll(inner, 1))
            return own + ends * near

        v = solve(r_v)
        w = solve(r_w)
        e = solve(r_e)
        vw_ref[0, :, cols] = jnp.where(row == 0, 1.0, v)
        vw_ref[1, :, cols] = jnp.where(row == 7, 1.0, w)
        diag = onto_ends(theta, e)
        cross = onto_ends(zero, w)
        mat = jnp.where(row == 0, diag, zero)
        mat = jnp.where(row == 1, roll(diag, 2), mat)
        mat = jnp.where(row == 2, roll(cross, 2), mat)
        mat = jnp.where(row == 3, roll(scaled, 3), mat)
        mat = jnp.where(row == 4, roll(scaled, 5), mat)
        send_ref[t, 24:32, :] = mat
        firsts, lasts, mixed = zero, zero, zero
        for j in range(comps):
            c = conc_ref[j, :, cols]
            g = solve(r_e * c)
            g_ref[j, :, cols] = g
            z = onto_ends(theta * c, g)
            if j < 8:
                z = roll(z, j) if j else z
                firsts = jnp.where(row == j, z, firsts)
                lasts = jnp.where(row == (j + 7) % 8, z, lasts)
            else:
                k = j - 8
                mixed = jnp.where(row == k, roll(z, k) if k else z, mixed)
                mixed = jnp.where(row == k + 4, roll(z, k + 5), mixed)
        send_ref[t, 0:8, :] = firsts
        send_ref[t, 8:16, :] = lasts
        send_ref[t, 16:24, :] = mixed

    def tiles_of(i, carry):
        for k in range(FEW):
            tile(i * FEW + k)
        return carry

    per = tiles // FEW // CHUNKS

    def chunk(n, carry):
        for copy in in_copies(n):
            copy.wait()
        lax.fori_loop(n * per, (n + 1) * per, tiles_of, 0)
        return carry

    lax.fori_loop(0, CHUNKS, chunk, 0)


FEW = 4


def first_row(j):
    return j if j < 8 else 16 + j - 8


def last_row(j):
    return 8 + (j + 7) % 8 if j < 8 else 20 + j - 8


def interface_kernel(recv_ref, active_ref, *refs):
    *surf_refs, ends_ref, top_ref = refs
    blocks = ends_ref.shape[0] // 24
    comps = 12
    shape = (blocks, LANES)
    row = rows_iota(shape)
    zero = jnp.zeros(shape, F32)

    def roll(v, d):
        return pltpu.roll(v, d % blocks, 0)

    def take(r):
        return recv_ref[pl.ds(r, blocks, stride=32), :]

    partial = tree_sum([ref[0] for ref in surf_refs])
    alpha = take(24) + jnp.where(row == 0, partial[comps : comps + 1], zero)
    beta, cross, s_first, s_last = take(25), take(26), take(27), take(28)
    s_above = roll(s_last, 1)
    link = 2.0 * s_above * s_first / (s_above + s_first)
    link = jnp.where((row > 0) & (8 * row < active_ref[...]), link, zero)
    wf = 1.0 / (alpha + cross + link)
    cross_w = cross * wf
    link_w = link * wf
    up = link * cross_w
    dn = roll(up, -1)
    excess = beta + alpha * cross_w + roll(alpha * link_w, -1)
    steps = []
    d = 1
    while d < blocks:
        w = 1.0 / (excess + up + dn)
        steps.append((d, up, dn, w))
        q = excess * w
        excess = excess + up * roll(q, d) + dn * roll(q, -d)
        up, dn = up * roll(up * w, d), dn * roll(dn * w, -d)
        d *= 2
    w_end = 1.0 / excess
    tops = []
    for j in range(comps):
        b = take(first_row(j)) + jnp.where(row == 0, partial[j : j + 1], zero)
        r = take(last_row(j)) + cross_w * b + roll(link_w * b, -1)
        for d, up, dn, w in steps:
            q = r * w
            r = r + up * roll(q, d) + dn * roll(q, -d)
        last = r * w_end
        first = link_w * roll(last, 1) + cross_w * last + wf * b
        ends_ref[pl.ds(j, blocks, stride=24), :] = first
        ends_ref[pl.ds(12 + j, blocks, stride=24), :] = last
        tops.append(first[0:1])
    top_ref[0] = jnp.concatenate(
        tops + [jnp.zeros((16 - comps, LANES), F32)], axis=0
    )


def lookup_kernel(table_ref, meta_ref, out_ref):
    table = table_ref[...]
    classes = table.shape[1]
    hi, mid, lo = split3(table)
    for t in range(out_ref.shape[0]):
        hit = (rows_iota((classes, LANES)) == meta_ref[t, 0:1, :]).astype(F32)
        hit = hit.astype(jnp.bfloat16)
        out_ref[t] = (
            jnp.dot(lo, hit, preferred_element_type=F32)
            + jnp.dot(mid, hit, preferred_element_type=F32)
            + jnp.dot(hi, hit, preferred_element_type=F32)
        )


LOG2E = 1.4426950408889634
LN2 = 0.6931471805599453


def tree_sum(terms):
    while len(terms) > 1:
        terms = [
            terms[i] + terms[i + 1] if i + 1 < len(terms) else terms[i]
            for i in range(0, len(terms), 2)
        ]
    return terms[0]


def speciate_kernel(
    g_ref, vw_ref, theta_ref, ends_ref, sorb_ref, log_ref, out_ref, sems
):
    comps = g_ref.shape[0]
    tiles = ends_ref.shape[0]
    each = range(comps)
    wide = tiles * LANES // CHUNKS

    def out_copy(n):
        part = pl.ds(pl.multiple_of(n * wide, wide), wide)
        return pltpu.make_async_copy(
            out_ref.at[:, :, part], log_ref.at[:, :, part], sems.at[n]
        )

    def tile(i, carry):
        group = [i * PAIR + k for k in range(PAIR)]
        cells = range(len(group))
        cols = [pl.ds(pl.multiple_of(t * LANES, LANES), LANES) for t in group]
        theta = [theta_ref[:, n] for n in cols]
        c = [[None] * comps for _ in cells]
        p = [[None] * comps for _ in cells]
        at = [[None] * comps for _ in cells]

        def aff(k, j):
            return sorb_ref[group[k], j : j + 1, :]

        cap = [sorb_ref[t, comps : comps + 1, :] for t in group]
        for j in each:
            for k in cells:
                total = (
                    g_ref[j, :, cols[k]]
                    + vw_ref[0, :, cols[k]] * ends_ref[group[k], j : j + 1, :]
                    + vw_ref[1, :, cols[k]] * ends_ref[group[k], 12 + j : 13 + j, :]
                )
                whole = theta[k] + cap[k] * aff(k, j)
                c[k][j] = total / whole
                p[k][j] = whole
                at[k][j] = aff(k, j) * total
        for step in range(ITERS):
            for k in cells:
                ac = [aff(k, j) * c[k][j] for j in each]
                load = tree_sum(ac)
                crowd = 1.0 + load
                hold = theta[k] * crowd
                q = [1.0 / (hold + cap[k] * aff(k, j)) for j in each]
                sum_c = tree_sum([ac[j] * q[j] for j in each])
                sum_t = tree_sum([at[k][j] * q[j] for j in each])
                lift = (load - crowd * sum_t) / (1.0 + hold * sum_c) * LOG2E
                crowd = crowd * LOG2E
                held = hold * lift
                lift = lift + LOG2E
                for j in each:
                    move = q[j] * (p[k][j] * crowd + held) - lift
                    move = jnp.clip(move, -LOG2E, LOG2E)
                    if step < ITERS - 1:
                        grow = jnp.exp2(move)
                        c[k][j] = c[k][j] * grow
                        p[k][j] = p[k][j] / grow
                    else:
                        out_ref[j, :, cols[k]] = jnp.log(c[k][j]) + move * LN2
        return carry

    per = tiles // PAIR // CHUNKS

    def chunk(n, carry):
        lax.fori_loop(n * per, (n + 1) * per, tile, 0)
        out_copy(n).start()
        return carry

    lax.fori_loop(0, CHUNKS, chunk, 0)
    for n in range(CHUNKS):
        out_copy(n).wait()


PAIR = 2
CHUNKS = 8


VMEM, HBM = pltpu.VMEM, pltpu.HBM


def full(memory_space=VMEM):
    return pl.BlockSpec(memory_space=memory_space)


def near(x):
    return x if INTERPRET else pltpu.with_memory_space_constraint(x, VMEM)


def far(x):
    return x if INTERPRET else pltpu.with_memory_space_constraint(x, HBM)


def held(shape):
    return jax.ShapeDtypeStruct(shape, F32) if INTERPRET else VMEM(shape, F32)


def swap(x, mask):
    n = lax.axis_size("grp")
    return lax.ppermute(x, "grp", [(i, i ^ mask) for i in range(n)])


def call(kernel, out_shape, n_in, **kw):
    n_out = len(out_shape) if isinstance(out_shape, (tuple, list)) else None
    out_specs = full() if n_out is None else tuple(full() for _ in range(n_out))
    inner = pl.pallas_call(
        kernel,
        out_shape=out_shape,
        in_specs=[full()] * n_in,
        out_specs=out_specs,
        interpret=INTERPRET,
        compiler_params=pltpu.CompilerParams(vmem_limit_bytes=24 << 20),
        **kw,
    )
    return lambda *args: inner(*(near(a) for a in args))


def exchange(x, axis):
    return lax.all_to_all(x, axis, split_axis=0, concat_axis=0, tiled=True)


def step(
    conc,
    porosity,
    cell_cond,
    soil_class,
    active,
    class_cond,
    sorb_affinity,
    sorb_capacity,
    surf_conc,
    surf_rate,
    surf_group,
    surf_local,
):
    groups = lax.axis_size("grp")
    owners = lax.axis_size("col")
    comps, depth, width = conc.shape
    n = surf_conc.shape[1]
    sds = jax.ShapeDtypeStruct
    first = (lax.axis_index("col") * depth).astype(jnp.int32).reshape(1)

    meta = pl.pallas_call(
        meta_kernel,
        out_shape=sds((owners, 2, LANES), jnp.int32),
        in_specs=[full()] * 2,
        out_specs=full(),
        interpret=INTERPRET,
        compiler_params=pltpu.CompilerParams(vmem_limit_bytes=24 << 20),
        name="meta",
    )(far(soil_class.reshape(1, LANES)), far(active.reshape(1, LANES)))
    meta = exchange(meta, "col")

    rate = surf_rate.reshape(1, n)
    group = surf_group.reshape(1, n)
    local = surf_local.reshape(1, n)
    smem = pl.BlockSpec(memory_space=pltpu.SMEM)
    me = lax.axis_index("grp").astype(jnp.int32).reshape(1)
    masks = halvings(groups)
    keep, surf_send = pl.pallas_call(
        surf_pack_kernel,
        out_shape=(
            sds((groups // 2, 16, LANES), F32),
            sds((groups // 2, 16, LANES), F32),
        ),
        in_specs=[smem] + [full()] * 4,
        out_specs=(full(), full()),
        scratch_shapes=[pltpu.VMEM((3, 16 * groups, n), jnp.bfloat16)],
        interpret=INTERPRET,
        compiler_params=pltpu.CompilerParams(vmem_limit_bytes=24 << 20),
        name="surf_pack",
    )(me, *(far(x) for x in (surf_conc, rate, group, local)))
    surf_parts = [keep]
    for k, mask in enumerate(masks):
        if k:
            surf_send = sum(x[mask : 2 * mask] for x in surf_parts)
        surf_parts.append(swap(surf_send, mask))
    surf_parts = [x[:1] for x in surf_parts]

    send, g, vw = pl.pallas_call(
        eliminate_kernel,
        out_shape=(
            held((owners, 32, LANES)),
            held((comps, depth, width)),
            held((2, depth, width)),
        ),
        in_specs=[smem, smem] + [pl.BlockSpec(memory_space=HBM)] * 3 + [full()],
        out_specs=(full(), full(), full()),
        scratch_shapes=[
            pltpu.VMEM((comps, depth, width), F32),
            pltpu.VMEM((depth, width), F32),
            pltpu.VMEM((depth, width), F32),
            pltpu.SemaphoreType.DMA((3 * CHUNKS,)),
        ],
        interpret=INTERPRET,
        compiler_params=pltpu.CompilerParams(vmem_limit_bytes=24 << 20),
        name="eliminate",
    )(first, far(class_cond), far(conc), far(porosity), far(cell_cond), near(meta))
    recv = exchange(send, "col")

    table = jnp.concatenate(
        [sorb_affinity.T, sorb_capacity[None], jnp.zeros((15 - comps, 16), F32)], axis=0
    )
    sorb = call(lookup_kernel, held((owners, 16, LANES)), 2, name="lookup")(table, meta)

    ends, top = call(
        interface_kernel,
        (held((owners * 24, LANES)), held((1, 16, LANES))),
        2 + len(surf_parts),
        name="interface",
    )(recv.reshape(owners * 32, LANES), active.reshape(1, LANES), *surf_parts)
    ends = exchange(ends.reshape(owners, 24, LANES), "col")
    for k, mask in enumerate(doublings(groups)):
        if k:
            top = jnp.concatenate([top, other], axis=0)
        other = swap(top, mask)

    log_free = pl.pallas_call(
        speciate_kernel,
        out_shape=sds((comps, depth, width), F32),
        in_specs=[full()] * 5,
        out_specs=pl.BlockSpec(memory_space=pl.ANY),
        scratch_shapes=[
            pltpu.VMEM((comps, depth, width), F32),
            pltpu.SemaphoreType.DMA((CHUNKS,)),
        ],
        interpret=INTERPRET,
        compiler_params=pltpu.CompilerParams(vmem_limit_bytes=24 << 20),
        name="speciate",
    )(near(g), near(vw), near(porosity), near(ends), near(sorb))

    flux = pl.pallas_call(
        surf_flux_kernel,
        out_shape=sds((comps, n), F32),
        in_specs=[smem] + [full()] * 6,
        out_specs=full(),
        interpret=INTERPRET,
        compiler_params=pltpu.CompilerParams(vmem_limit_bytes=24 << 20),
        name="surf_flux",
    )(me, near(top), near(other), *(near(x) for x in (surf_conc, rate, group, local)))
    return (log_free, flux)


def solution(mesh):
    return jax.shard_map(
        step,
        mesh=mesh,
        in_specs=(
            P(None, "col", "grp"),
            P("col", "grp"),
            P("col", "grp"),
            P(("grp", "col")),
            P(("grp", "col")),
            P(),
            P(),
            P(),
            P(None, ("grp", "col")),
            P(("grp", "col")),
            P(("grp", "col"), None),
            P(("grp", "col")),
        ),
        out_specs=(P(None, "col", "grp"), P(None, ("grp", "col"))),
        check_vma=False,
    )
```

```python
import jax
import jax.numpy as jnp
from jax import lax
from jax.experimental import pallas as pl
from jax.experimental.pallas import tpu as pltpu
from jax.sharding import PartitionSpec as P

ITERS = 4
LANES = 128
F32 = jnp.float32
INTERPRET = False


def split3(v):
    hi = v.astype(jnp.bfloat16)
    rest = v - hi.astype(F32)
    mid = rest.astype(jnp.bfloat16)
    lo = (rest - mid.astype(F32)).astype(jnp.bfloat16)
    return hi, mid, lo


def rows_iota(shape):
    return lax.broadcasted_iota(jnp.int32, shape, 0)


def meta_kernel(class_ref, active_ref, out_ref):
    both = jnp.concatenate([class_ref[...], active_ref[...]], axis=0)
    for t in range(out_ref.shape[0]):
        out_ref[t] = both


def surf_pack_kernel(
    me_ref, conc_ref, rate_ref, group_ref, local_ref, keep_ref, send_ref, lhs_ref
):
    comps, n = conc_ref.shape
    half = send_ref.shape[0]
    rate = rate_ref[...]
    vals = jnp.concatenate(
        [conc_ref[...] * rate, rate, jnp.zeros((15 - comps, n), F32)], axis=0
    )
    parts = [part.astype(F32) for part in split3(vals)]
    slot = group_ref[...] ^ me_ref[0]
    for b in range(2 * half):
        keep = slot == b
        for i, part in enumerate(parts):
            lhs_ref[i, 16 * b : 16 * b + 16, :] = jnp.where(keep, part, 0.0).astype(
                jnp.bfloat16
            )
    place = (rows_iota((LANES, n)) == local_ref[...]).astype(F32).astype(jnp.bfloat16)
    dims = (((1,), (1,)), ((), ()))
    total = sum(
        lax.dot_general(lhs_ref[i], place, dims, preferred_element_type=F32)
        for i in (2, 1, 0)
    )
    total = total.reshape(2 * half, 16, LANES)
    keep_ref[...] = total[:half]
    send_ref[...] = total[half:]


def surf_flux_kernel(
    me_ref, near_ref, far_ref, conc_ref, rate_ref, group_ref, local_ref, flux_ref
):
    comps, n = conc_ref.shape
    half = far_ref.shape[0]
    place = (rows_iota((LANES, n)) == local_ref[...]).astype(F32).astype(jnp.bfloat16)
    table = jnp.concatenate([near_ref[...], far_ref[...]], axis=0)
    hi, mid, lo = split3(table.reshape(2 * half * 16, LANES))
    picked = jnp.dot(lo, place, preferred_element_type=F32)
    picked += jnp.dot(mid, place, preferred_element_type=F32)
    picked += jnp.dot(hi, place, preferred_element_type=F32)
    slot = group_ref[...] ^ me_ref[0]
    top = jnp.zeros((16, n), F32)
    for i in range(2 * half):
        top = jnp.where(slot == slot_mask(i, 2 * half), picked[16 * i : 16 * i + 16], top)
    rate = rate_ref[...]
    flux_ref[...] = rate * conc_ref[...] - rate * top[:comps]


def halvings(n):
    masks = []
    while n > 1:
        n //= 2
        masks.append(n)
    return masks


def doublings(n):
    masks = halvings(n)
    return [masks[k] for k in (0, 3, 2, 1) if k < len(masks)]


def slot_mask(i, n):
    return sum(m for k, m in enumerate(doublings(n)) if i >> k & 1)


def eliminate_kernel(
    first_ref,
    table_ref,
    conc_hbm,
    theta_hbm,
    cond_hbm,
    meta_ref,
    send_ref,
    g_ref,
    vw_ref,
    conc_ref,
    theta_ref,
    cond_ref,
    sems,
):
    comps = conc_ref.shape[0]
    wide = conc_ref.shape[2] // CHUNKS

    def in_copies(n):
        part = pl.ds(pl.multiple_of(n * wide, wide), wide)
        return [
            pltpu.make_async_copy(
                theta_hbm.at[:, part], theta_ref.at[:, part], sems.at[3 * n]
            ),
            pltpu.make_async_copy(
                cond_hbm.at[:, part], cond_ref.at[:, part], sems.at[3 * n + 1]
            ),
            pltpu.make_async_copy(
                conc_hbm.at[:, :, part], conc_ref.at[:, :, part], sems.at[3 * n + 2]
            ),
        ]

    for n in range(CHUNKS):
        for copy in in_copies(n):
            copy.start()
    tiles = send_ref.shape[0] // ROWS
    shape = (8, LANES)
    row = rows_iota(shape)
    zero = jnp.zeros(shape, F32)
    layer = first_ref[0] + row

    def roll(v, d):
        return pltpu.roll(v, d % 8, 0)

    def tile(t):
        cols = pl.ds(pl.multiple_of(t * LANES, LANES), LANES)
        classes = meta_ref[t, 0:1, :]
        active = meta_ref[t, 1:2, :]
        scale = jnp.zeros((1, LANES), F32)
        for k in range(table_ref.shape[0]):
            scale = jnp.where(classes == k, table_ref[k], scale)
        theta = theta_ref[:, cols]
        scaled = cond_ref[:, cols] * scale
        below = roll(scaled, -1)
        link = 2.0 * scaled * below / (scaled + below)
        link = jnp.where((row < 7) & (layer + 1 < active), link, zero)
        link_up = roll(link, 1)
        up = jnp.where(row >= 2, link_up, zero)
        dn = jnp.where(row <= 5, link, zero)
        r_v = jnp.where(row == 1, link_up, zero)
        r_w = jnp.where(row == 6, link, zero)
        excess = theta + r_v + r_w
        w1 = 1.0 / (excess + up + dn)
        t1 = excess * w1
        up1, dn1 = up, dn
        excess = excess + up * roll(t1, 1) + dn * roll(t1, -1)
        up2 = up * roll(up * w1, 1)
        dn2 = dn * roll(dn * w1, -1)
        w2 = 1.0 / (excess + up2 + dn2)
        t2 = excess * w2
        excess = excess + up2 * roll(t2, 2) + dn2 * roll(t2, -2)
        up3 = up2 * roll(up2 * w2, 2)
        dn3 = dn2 * roll(dn2 * w2, -2)
        far = up3 + dn3
        w3 = 1.0 / (excess + far)
        excess = excess + far * roll(excess * w3, 4)
        inner = (row >= 1) & (row <= 6)
        w4 = jnp.where(inner, 1.0 / excess, 1.0)

        def solve(r):
            q = r * w1
            r = r + up1 * roll(q, 1) + dn1 * roll(q, -1)
            q = r * w2
            r = r + up2 * roll(q, 2) + dn2 * roll(q, -2)
            r = r + far * roll(r * w3, 4)
            return r * w4

        def put(r, value, layer):
            send_ref[pl.ds(t * ROWS + r, 1), :] = value[layer : layer + 1]

        v = solve(r_v)
        w = solve(r_w)
        e = solve(theta)
        vw_ref[0, :, cols] = jnp.where(row == 0, 1.0, jnp.where(inner, v, zero))
        vw_ref[1, :, cols] = jnp.where(row == 7, 1.0, jnp.where(inner, w, zero))
        put(24, e, 0)
        put(25, e, 7)
        put(26, w, 0)
        put(27, scaled, 0)
        put(28, scaled, 7)
        for j in range(comps):
            x = solve(theta * conc_ref[j, :, cols])
            g_ref[j, :, cols] = jnp.where(inner, x, zero)
            put(j, x, 0)
            put(12 + j, x, 7)

    def tiles_of(i, carry):
        for k in range(FEW):
            tile(i * FEW + k)
        return carry

    per = tiles // FEW // CHUNKS

    def chunk(n, carry):
        for copy in in_copies(n):
            copy.wait()
        lax.fori_loop(n * per, (n + 1) * per, tiles_of, 0)
        return carry

    lax.fori_loop(0, CHUNKS, chunk, 0)


FEW = 4
ROWS = 29


def interface_kernel(recv_ref, active_ref, *refs):
    *surf_refs, ends_ref, top_ref = refs
    blocks = ends_ref.shape[0] // 24
    comps = 12
    shape = (blocks, LANES)
    row = rows_iota(shape)
    zero = jnp.zeros(shape, F32)

    def roll(v, d):
        return pltpu.roll(v, d % blocks, 0)

    def take(r):
        return recv_ref[pl.ds(r, blocks, stride=ROWS), :]

    partial = tree_sum([ref[0] for ref in surf_refs])
    alpha = take(24) + jnp.where(row == 0, partial[comps : comps + 1], zero)
    beta, cross, s_first, s_last = take(25), take(26), take(27), take(28)
    s_above = roll(s_last, 1)
    link = 2.0 * s_above * s_first / (s_above + s_first)
    link = jnp.where((row > 0) & (8 * row < active_ref[...]), link, zero)
    wf = 1.0 / (alpha + cross + link)
    cross_w = cross * wf
    link_w = link * wf
    up = link * cross_w
    dn = roll(up, -1)
    excess = beta + alpha * cross_w + roll(alpha * link_w, -1)
    steps = []
    d = 1
    while d < blocks:
        w = 1.0 / (excess + up + dn)
        steps.append((d, up, dn, w))
        q = excess * w
        excess = excess + up * roll(q, d) + dn * roll(q, -d)
        up, dn = up * roll(up * w, d), dn * roll(dn * w, -d)
        d *= 2
    w_end = 1.0 / excess
    tops = []
    for j in range(comps):
        b = take(j) + jnp.where(row == 0, partial[j : j + 1], zero)
        r = take(12 + j) + cross_w * b + roll(link_w * b, -1)
        for d, up, dn, w in steps:
            q = r * w
            r = r + up * roll(q, d) + dn * roll(q, -d)
        last = r * w_end
        first = link_w * roll(last, 1) + cross_w * last + wf * b
        ends_ref[pl.ds(j, blocks, stride=24), :] = first
        ends_ref[pl.ds(12 + j, blocks, stride=24), :] = last
        tops.append(first[0:1])
    top_ref[0] = jnp.concatenate(
        tops + [jnp.zeros((16 - comps, LANES), F32)], axis=0
    )


def lookup_kernel(table_ref, meta_ref, out_ref):
    table = table_ref[...]
    classes = table.shape[1]
    hi, mid, lo = split3(table)
    for t in range(out_ref.shape[0]):
        hit = (rows_iota((classes, LANES)) == meta_ref[t, 0:1, :]).astype(F32)
        hit = hit.astype(jnp.bfloat16)
        out_ref[t] = (
            jnp.dot(lo, hit, preferred_element_type=F32)
            + jnp.dot(mid, hit, preferred_element_type=F32)
            + jnp.dot(hi, hit, preferred_element_type=F32)
        )


LOG2E = 1.4426950408889634
LN2 = 0.6931471805599453


def tree_sum(terms):
    while len(terms) > 1:
        terms = [
            terms[i] + terms[i + 1] if i + 1 < len(terms) else terms[i]
            for i in range(0, len(terms), 2)
        ]
    return terms[0]


def speciate_kernel(
    g_ref, vw_ref, theta_ref, ends_ref, sorb_ref, log_ref, out_ref, sems
):
    comps = g_ref.shape[0]
    tiles = ends_ref.shape[0]
    each = range(comps)
    wide = tiles * LANES // CHUNKS

    def out_copy(n):
        part = pl.ds(pl.multiple_of(n * wide, wide), wide)
        return pltpu.make_async_copy(
            out_ref.at[:, :, part], log_ref.at[:, :, part], sems.at[n]
        )

    def tile(i, carry):
        group = [i * PAIR + k for k in range(PAIR)]
        cells = range(len(group))
        cols = [pl.ds(pl.multiple_of(t * LANES, LANES), LANES) for t in group]
        theta = [theta_ref[:, n] for n in cols]
        c = [[None] * comps for _ in cells]
        p = [[None] * comps for _ in cells]
        at = [[None] * comps for _ in cells]

        def aff(k, j):
            return sorb_ref[group[k], j : j + 1, :]

        cap = [sorb_ref[t, comps : comps + 1, :] for t in group]
        for j in each:
            for k in cells:
                total = (
                    g_ref[j, :, cols[k]]
                    + vw_ref[0, :, cols[k]] * ends_ref[group[k], j : j + 1, :]
                    + vw_ref[1, :, cols[k]] * ends_ref[group[k], 12 + j : 13 + j, :]
                )
                whole = theta[k] + cap[k] * aff(k, j)
                c[k][j] = total / whole
                p[k][j] = whole
                at[k][j] = aff(k, j) * total
        for step in range(ITERS):
            for k in cells:
                ac = [aff(k, j) * c[k][j] for j in each]
                load = tree_sum(ac)
                crowd = 1.0 + load
                hold = theta[k] * crowd
                q = [1.0 / (hold + cap[k] * aff(k, j)) for j in each]
                sum_c = tree_sum([ac[j] * q[j] for j in each])
                sum_t = tree_sum([at[k][j] * q[j] for j in each])
                lift = (load - crowd * sum_t) / (1.0 + hold * sum_c) * LOG2E
                crowd = crowd * LOG2E
                held = hold * lift
                lift = lift + LOG2E
                for j in each:
                    move = q[j] * (p[k][j] * crowd + held) - lift
                    move = jnp.clip(move, -LOG2E, LOG2E)
                    if step < ITERS - 1:
                        grow = jnp.exp2(move)
                        c[k][j] = c[k][j] * grow
                        p[k][j] = p[k][j] / grow
                    else:
                        out_ref[j, :, cols[k]] = jnp.log(c[k][j]) + move * LN2
        return carry

    per = tiles // PAIR // CHUNKS

    def chunk(n, carry):
        lax.fori_loop(n * per, (n + 1) * per, tile, 0)
        out_copy(n).start()
        return carry

    lax.fori_loop(0, CHUNKS, chunk, 0)
    for n in range(CHUNKS):
        out_copy(n).wait()


PAIR = 2
CHUNKS = 8


VMEM, HBM = pltpu.VMEM, pltpu.HBM


def full(memory_space=VMEM):
    return pl.BlockSpec(memory_space=memory_space)


def near(x):
    return x if INTERPRET else pltpu.with_memory_space_constraint(x, VMEM)


def far(x):
    return x if INTERPRET else pltpu.with_memory_space_constraint(x, HBM)


def held(shape):
    return jax.ShapeDtypeStruct(shape, F32) if INTERPRET else VMEM(shape, F32)


def swap(x, mask):
    n = lax.axis_size("grp")
    return lax.ppermute(x, "grp", [(i, i ^ mask) for i in range(n)])


def call(kernel, out_shape, n_in, **kw):
    n_out = len(out_shape) if isinstance(out_shape, (tuple, list)) else None
    out_specs = full() if n_out is None else tuple(full() for _ in range(n_out))
    inner = pl.pallas_call(
        kernel,
        out_shape=out_shape,
        in_specs=[full()] * n_in,
        out_specs=out_specs,
        interpret=INTERPRET,
        compiler_params=pltpu.CompilerParams(vmem_limit_bytes=24 << 20),
        **kw,
    )
    return lambda *args: inner(*(near(a) for a in args))


def exchange(x, axis):
    return lax.all_to_all(x, axis, split_axis=0, concat_axis=0, tiled=True)


def step(
    conc,
    porosity,
    cell_cond,
    soil_class,
    active,
    class_cond,
    sorb_affinity,
    sorb_capacity,
    surf_conc,
    surf_rate,
    surf_group,
    surf_local,
):
    groups = lax.axis_size("grp")
    owners = lax.axis_size("col")
    comps, depth, width = conc.shape
    n = surf_conc.shape[1]
    sds = jax.ShapeDtypeStruct
    first = (lax.axis_index("col") * depth).astype(jnp.int32).reshape(1)

    meta = pl.pallas_call(
        meta_kernel,
        out_shape=sds((owners, 2, LANES), jnp.int32),
        in_specs=[full()] * 2,
        out_specs=full(),
        interpret=INTERPRET,
        compiler_params=pltpu.CompilerParams(vmem_limit_bytes=24 << 20),
        name="meta",
    )(far(soil_class.reshape(1, LANES)), far(active.reshape(1, LANES)))
    meta = exchange(meta, "col")

    rate = surf_rate.reshape(1, n)
    group = surf_group.reshape(1, n)
    local = surf_local.reshape(1, n)
    smem = pl.BlockSpec(memory_space=pltpu.SMEM)
    me = lax.axis_index("grp").astype(jnp.int32).reshape(1)
    masks = halvings(groups)
    keep, surf_send = pl.pallas_call(
        surf_pack_kernel,
        out_shape=(
            sds((groups // 2, 16, LANES), F32),
            sds((groups // 2, 16, LANES), F32),
        ),
        in_specs=[smem] + [full()] * 4,
        out_specs=(full(), full()),
        scratch_shapes=[pltpu.VMEM((3, 16 * groups, n), jnp.bfloat16)],
        interpret=INTERPRET,
        compiler_params=pltpu.CompilerParams(vmem_limit_bytes=24 << 20),
        name="surf_pack",
    )(me, *(far(x) for x in (surf_conc, rate, group, local)))
    surf_parts = [keep]
    for k, mask in enumerate(masks):
        if k:
            surf_send = sum(x[mask : 2 * mask] for x in surf_parts)
        surf_parts.append(swap(surf_send, mask))
    surf_parts = [x[:1] for x in surf_parts]

    send, g, vw = pl.pallas_call(
        eliminate_kernel,
        out_shape=(
            held((owners * ROWS, LANES)),
            held((comps, depth, width)),
            held((2, depth, width)),
        ),
        in_specs=[smem, smem] + [pl.BlockSpec(memory_space=HBM)] * 3 + [full()],
        out_specs=(full(), full(), full()),
        scratch_shapes=[
            pltpu.VMEM((comps, depth, width), F32),
            pltpu.VMEM((depth, width), F32),
            pltpu.VMEM((depth, width), F32),
            pltpu.SemaphoreType.DMA((3 * CHUNKS,)),
        ],
        interpret=INTERPRET,
        compiler_params=pltpu.CompilerParams(vmem_limit_bytes=24 << 20),
        name="eliminate",
    )(first, far(class_cond), far(conc), far(porosity), far(cell_cond), near(meta))
    recv = exchange(send.reshape(owners, ROWS, 1, LANES), "col")

    table = jnp.concatenate(
        [sorb_affinity.T, sorb_capacity[None], jnp.zeros((15 - comps, 16), F32)], axis=0
    )
    sorb = call(lookup_kernel, held((owners, 16, LANES)), 2, name="lookup")(table, meta)

    ends, top = call(
        interface_kernel,
        (held((owners * 24, LANES)), held((1, 16, LANES))),
        2 + len(surf_parts),
        name="interface",
    )(recv.reshape(owners * ROWS, LANES), active.reshape(1, LANES), *surf_parts)
    ends = exchange(ends.reshape(owners, 24, LANES), "col")
    for k, mask in enumerate(doublings(groups)):
        if k:
            top = jnp.concatenate([top, other], axis=0)
        other = swap(top, mask)

    log_free = pl.pallas_call(
        speciate_kernel,
        out_shape=sds((comps, depth, width), F32),
        in_specs=[full()] * 5,
        out_specs=pl.BlockSpec(memory_space=pl.ANY),
        scratch_shapes=[
            pltpu.VMEM((comps, depth, width), F32),
            pltpu.SemaphoreType.DMA((CHUNKS,)),
        ],
        interpret=INTERPRET,
        compiler_params=pltpu.CompilerParams(vmem_limit_bytes=24 << 20),
        name="speciate",
    )(near(g), near(vw), near(porosity), near(ends), near(sorb))

    flux = pl.pallas_call(
        surf_flux_kernel,
        out_shape=sds((comps, n), F32),
        in_specs=[smem] + [full()] * 6,
        out_specs=full(),
        interpret=INTERPRET,
        compiler_params=pltpu.CompilerParams(vmem_limit_bytes=24 << 20),
        name="surf_flux",
    )(me, near(top), near(other), *(near(x) for x in (surf_conc, rate, group, local)))
    return (log_free, flux)


def solution(mesh):
    return jax.shard_map(
        step,
        mesh=mesh,
        in_specs=(
            P(None, "col", "grp"),
            P("col", "grp"),
            P("col", "grp"),
            P(("grp", "col")),
            P(("grp", "col")),
            P(),
            P(),
            P(),
            P(None, ("grp", "col")),
            P(("grp", "col")),
            P(("grp", "col"), None),
            P(("grp", "col")),
        ),
        out_specs=(P(None, "col", "grp"), P(None, ("grp", "col"))),
        check_vma=False,
    )
```

```python
import jax
import jax.numpy as jnp
from jax import lax
from jax.experimental import pallas as pl
from jax.experimental.pallas import tpu as pltpu
from jax.sharding import PartitionSpec as P

ITERS = 4
LANES = 128
F32 = jnp.float32
INTERPRET = False


def split3(v):
    hi = v.astype(jnp.bfloat16)
    rest = v - hi.astype(F32)
    mid = rest.astype(jnp.bfloat16)
    lo = (rest - mid.astype(F32)).astype(jnp.bfloat16)
    return hi, mid, lo


def rows_iota(shape):
    return lax.broadcasted_iota(jnp.int32, shape, 0)


def meta_kernel(class_ref, active_ref, out_ref):
    both = jnp.concatenate([class_ref[...], active_ref[...]], axis=0)
    for t in range(out_ref.shape[0]):
        out_ref[t] = both


def surf_pack_kernel(
    me_ref, conc_ref, rate_ref, group_ref, local_ref, *refs
):
    brick_hbm, refs = refs[:3], refs[3:]
    keep_ref, send_ref, *brick, lhs_ref, sems = refs
    copies = [
        pltpu.make_async_copy(brick_hbm[k], brick[k], sems.at[k]) for k in range(3)
    ]
    for copy in copies:
        copy.start()
    comps, n = conc_ref.shape
    half = send_ref.shape[0]
    rate = rate_ref[...]
    vals = jnp.concatenate(
        [conc_ref[...] * rate, rate, jnp.zeros((15 - comps, n), F32)], axis=0
    )
    parts = [part.astype(F32) for part in split3(vals)]
    slot = group_ref[...] ^ me_ref[0]
    for b in range(2 * half):
        keep = slot == half_mask(b, 2 * half)
        for i, part in enumerate(parts):
            lhs_ref[i, 16 * b : 16 * b + 16, :] = jnp.where(keep, part, 0.0).astype(
                jnp.bfloat16
            )
    place = (rows_iota((LANES, n)) == local_ref[...]).astype(F32).astype(jnp.bfloat16)
    dims = (((1,), (1,)), ((), ()))
    total = sum(
        lax.dot_general(lhs_ref[i], place, dims, preferred_element_type=F32)
        for i in (2, 1, 0)
    )
    total = total.reshape(2 * half, 16, LANES)
    keep_ref[...] = total[:half]
    send_ref[...] = total[half:]
    for copy in copies:
        copy.wait()


def surf_flux_kernel(
    me_ref, near_ref, far_ref, conc_ref, rate_ref, group_ref, local_ref, flux_ref
):
    comps, n = conc_ref.shape
    half = far_ref.shape[0]
    place = (rows_iota((LANES, n)) == local_ref[...]).astype(F32).astype(jnp.bfloat16)
    table = jnp.concatenate([near_ref[...], far_ref[...]], axis=0)
    hi, mid, lo = split3(table.reshape(2 * half * 16, LANES))
    picked = jnp.dot(lo, place, preferred_element_type=F32)
    picked += jnp.dot(mid, place, preferred_element_type=F32)
    picked += jnp.dot(hi, place, preferred_element_type=F32)
    slot = group_ref[...] ^ me_ref[0]
    top = jnp.zeros((16, n), F32)
    for i in range(2 * half):
        top = jnp.where(slot == slot_mask(i, 2 * half), picked[16 * i : 16 * i + 16], top)
    rate = rate_ref[...]
    flux_ref[...] = rate * conc_ref[...] - rate * top[:comps]


def halvings(n):
    masks = []
    while n > 1:
        n //= 2
        masks.append(n)
    return masks


def partners(n):
    masks = halvings(n)
    return [masks[k] for k in (3, 0, 2, 1) if k < len(masks)]


def half_mask(b, n):
    return sum(p for m, p in zip(halvings(n), partners(n)) if b & m)


def doublings(n):
    masks = halvings(n)
    return [masks[k] for k in (0, 3, 2, 1) if k < len(masks)]


def slot_mask(i, n):
    return sum(m for k, m in enumerate(doublings(n)) if i >> k & 1)


def eliminate_kernel(
    first_ref,
    table_ref,
    conc_ref,
    theta_ref,
    cond_ref,
    meta_ref,
    send_ref,
    g_ref,
    vw_ref,
):
    comps = conc_ref.shape[0]
    tiles = send_ref.shape[0] // ROWS
    shape = (8, LANES)
    row = rows_iota(shape)
    zero = jnp.zeros(shape, F32)
    layer = first_ref[0] + row

    def roll(v, d):
        return pltpu.roll(v, d % 8, 0)

    def read(t):
        cols = pl.ds(pl.multiple_of(t * LANES, LANES), LANES)
        return [conc_ref[j, :, cols] for j in range(comps)]

    def tile(t, conc):
        cols = pl.ds(pl.multiple_of(t * LANES, LANES), LANES)
        classes = meta_ref[t, 0:1, :]
        active = meta_ref[t, 1:2, :]
        scale = jnp.zeros((1, LANES), F32)
        for k in range(table_ref.shape[0]):
            scale = jnp.where(classes == k, table_ref[k], scale)
        theta = theta_ref[:, cols]
        scaled = cond_ref[:, cols] * scale
        below = roll(scaled, -1)
        link = 2.0 * scaled * below / (scaled + below)
        link = jnp.where((row < 7) & (layer + 1 < active), link, zero)
        link_up = roll(link, 1)
        up = jnp.where(row >= 2, link_up, zero)
        dn = jnp.where(row <= 5, link, zero)
        r_v = jnp.where(row == 1, link_up, zero)
        r_w = jnp.where(row == 6, link, zero)
        excess = theta + r_v + r_w
        w1 = 1.0 / (excess + up + dn)
        t1 = excess * w1
        up1, dn1 = up, dn
        excess = excess + up * roll(t1, 1) + dn * roll(t1, -1)
        up2 = up * roll(up * w1, 1)
        dn2 = dn * roll(dn * w1, -1)
        w2 = 1.0 / (excess + up2 + dn2)
        t2 = excess * w2
        excess = excess + up2 * roll(t2, 2) + dn2 * roll(t2, -2)
        up3 = up2 * roll(up2 * w2, 2)
        dn3 = dn2 * roll(dn2 * w2, -2)
        far = up3 + dn3
        w3 = 1.0 / (excess + far)
        excess = excess + far * roll(excess * w3, 4)
        inner = (row >= 1) & (row <= 6)
        w4 = jnp.where(inner, 1.0 / excess, 1.0)

        def solve(r):
            q = r * w1
            r = r + up1 * roll(q, 1) + dn1 * roll(q, -1)
            q = r * w2
            r = r + up2 * roll(q, 2) + dn2 * roll(q, -2)
            r = r + far * roll(r * w3, 4)
            return r * w4

        def put(r, value, layer):
            send_ref[pl.ds(t * ROWS + r, 1), :] = value[layer : layer + 1]

        v = solve(r_v)
        w = solve(r_w)
        e = solve(theta)
        vw_ref[0, :, cols] = jnp.where(row == 0, 1.0, jnp.where(inner, v, zero))
        vw_ref[1, :, cols] = jnp.where(row == 7, 1.0, jnp.where(inner, w, zero))
        put(24, e, 0)
        put(25, e, 7)
        put(26, w, 0)
        put(27, scaled, 0)
        put(28, scaled, 7)
        found = []
        for j in range(comps):
            x = solve(theta * conc[j])
            found.append(jnp.where(inner, x, zero))
            put(j, x, 0)
            put(12 + j, x, 7)
        return cols, found

    def tiles_of(i, carry):
        group = [i * FEW + k for k in range(FEW)]
        conc = [read(t) for t in group]
        done = [tile(t, c) for t, c in zip(group, conc)]
        for cols, found in done:
            for j in range(comps):
                g_ref[j, :, cols] = found[j]
        return carry

    lax.fori_loop(0, tiles // FEW, tiles_of, 0)


FEW = 4
ROWS = 29


def interface_kernel(recv_ref, active_ref, *refs):
    *surf_refs, ends_ref, top_ref = refs
    blocks = ends_ref.shape[0] // 24
    comps = 12
    shape = (blocks, LANES)
    row = rows_iota(shape)
    zero = jnp.zeros(shape, F32)

    def roll(v, d):
        return pltpu.roll(v, d % blocks, 0)

    def take(r):
        return recv_ref[pl.ds(r, blocks, stride=ROWS), :]

    partial = tree_sum([ref[0] for ref in surf_refs])
    alpha = take(24) + jnp.where(row == 0, partial[comps : comps + 1], zero)
    beta, cross, s_first, s_last = take(25), take(26), take(27), take(28)
    s_above = roll(s_last, 1)
    link = 2.0 * s_above * s_first / (s_above + s_first)
    link = jnp.where((row > 0) & (8 * row < active_ref[...]), link, zero)
    wf = 1.0 / (alpha + cross + link)
    cross_w = cross * wf
    link_w = link * wf
    up = link * cross_w
    dn = roll(up, -1)
    excess = beta + alpha * cross_w + roll(alpha * link_w, -1)
    steps = []
    d = 1
    while d < blocks:
        w = 1.0 / (excess + up + dn)
        steps.append((d, up, dn, w))
        q = excess * w
        excess = excess + up * roll(q, d) + dn * roll(q, -d)
        up, dn = up * roll(up * w, d), dn * roll(dn * w, -d)
        d *= 2
    w_end = 1.0 / excess
    tops = []
    for j in range(comps):
        b = take(j) + jnp.where(row == 0, partial[j : j + 1], zero)
        r = take(12 + j) + cross_w * b + roll(link_w * b, -1)
        for d, up, dn, w in steps:
            q = r * w
            r = r + up * roll(q, d) + dn * roll(q, -d)
        last = r * w_end
        first = link_w * roll(last, 1) + cross_w * last + wf * b
        ends_ref[pl.ds(j, blocks, stride=24), :] = first
        ends_ref[pl.ds(12 + j, blocks, stride=24), :] = last
        tops.append(first[0:1])
    top_ref[0] = jnp.concatenate(
        tops + [jnp.zeros((16 - comps, LANES), F32)], axis=0
    )


def lookup_kernel(table_ref, meta_ref, out_ref):
    table = table_ref[...]
    classes = table.shape[1]
    hi, mid, lo = split3(table)
    for t in range(out_ref.shape[0]):
        hit = (rows_iota((classes, LANES)) == meta_ref[t, 0:1, :]).astype(F32)
        hit = hit.astype(jnp.bfloat16)
        out_ref[t] = (
            jnp.dot(lo, hit, preferred_element_type=F32)
            + jnp.dot(mid, hit, preferred_element_type=F32)
            + jnp.dot(hi, hit, preferred_element_type=F32)
        )


LOG2E = 1.4426950408889634
LN2 = 0.6931471805599453


def tree_sum(terms):
    while len(terms) > 1:
        terms = [
            terms[i] + terms[i + 1] if i + 1 < len(terms) else terms[i]
            for i in range(0, len(terms), 2)
        ]
    return terms[0]


def speciate_kernel(
    g_ref, vw_ref, theta_ref, ends_ref, sorb_ref, log_ref, out_ref, sems
):
    comps = g_ref.shape[0]
    tiles = ends_ref.shape[0]
    each = range(comps)
    wide = tiles * LANES // CHUNKS

    def out_copy(n):
        part = pl.ds(pl.multiple_of(n * wide, wide), wide)
        return pltpu.make_async_copy(
            out_ref.at[:, :, part], log_ref.at[:, :, part], sems.at[n]
        )

    def tile(i, carry):
        group = [i * PAIR + k for k in range(PAIR)]
        cells = range(len(group))
        cols = [pl.ds(pl.multiple_of(t * LANES, LANES), LANES) for t in group]
        theta = [theta_ref[:, n] for n in cols]
        c = [[None] * comps for _ in cells]
        p = [[None] * comps for _ in cells]
        at = [[None] * comps for _ in cells]

        def aff(k, j):
            return sorb_ref[group[k], j : j + 1, :]

        cap = [sorb_ref[t, comps : comps + 1, :] for t in group]
        for j in each:
            for k in cells:
                total = (
                    g_ref[j, :, cols[k]]
                    + vw_ref[0, :, cols[k]] * ends_ref[group[k], j : j + 1, :]
                    + vw_ref[1, :, cols[k]] * ends_ref[group[k], 12 + j : 13 + j, :]
                )
                whole = theta[k] + cap[k] * aff(k, j)
                c[k][j] = total / whole
                p[k][j] = whole
                at[k][j] = aff(k, j) * total
        for step in range(ITERS):
            for k in cells:
                ac = [aff(k, j) * c[k][j] for j in each]
                load = tree_sum(ac)
                crowd = 1.0 + load
                hold = theta[k] * crowd
                q = [1.0 / (hold + cap[k] * aff(k, j)) for j in each]
                sum_c = tree_sum([ac[j] * q[j] for j in each])
                sum_t = tree_sum([at[k][j] * q[j] for j in each])
                lift = (load - crowd * sum_t) / (1.0 + hold * sum_c) * LOG2E
                crowd = crowd * LOG2E
                held = hold * lift
                lift = lift + LOG2E
                for j in each:
                    move = q[j] * (p[k][j] * crowd + held) - lift
                    move = jnp.clip(move, -LOG2E, LOG2E)
                    if step < ITERS - 1:
                        grow = jnp.exp2(move)
                        c[k][j] = c[k][j] * grow
                        p[k][j] = p[k][j] / grow
                    else:
                        out_ref[j, :, cols[k]] = jnp.log(c[k][j]) + move * LN2
        return carry

    per = tiles // PAIR // CHUNKS

    def chunk(n, carry):
        lax.fori_loop(n * per, (n + 1) * per, tile, 0)
        out_copy(n).start()
        return carry

    lax.fori_loop(0, CHUNKS, chunk, 0)
    for n in range(CHUNKS):
        out_copy(n).wait()


PAIR = 2
CHUNKS = 8


VMEM, HBM = pltpu.VMEM, pltpu.HBM


def full(memory_space=VMEM):
    return pl.BlockSpec(memory_space=memory_space)


def near(x):
    return x if INTERPRET else pltpu.with_memory_space_constraint(x, VMEM)


def far(x):
    return x if INTERPRET else pltpu.with_memory_space_constraint(x, HBM)


def held(shape):
    return jax.ShapeDtypeStruct(shape, F32) if INTERPRET else VMEM(shape, F32)


def swap(x, mask):
    n = lax.axis_size("grp")
    return lax.ppermute(x, "grp", [(i, i ^ mask) for i in range(n)])


def call(kernel, out_shape, n_in, **kw):
    n_out = len(out_shape) if isinstance(out_shape, (tuple, list)) else None
    out_specs = full() if n_out is None else tuple(full() for _ in range(n_out))
    inner = pl.pallas_call(
        kernel,
        out_shape=out_shape,
        in_specs=[full()] * n_in,
        out_specs=out_specs,
        interpret=INTERPRET,
        compiler_params=pltpu.CompilerParams(vmem_limit_bytes=24 << 20),
        **kw,
    )
    return lambda *args: inner(*(near(a) for a in args))


def exchange(x, axis):
    return lax.all_to_all(x, axis, split_axis=0, concat_axis=0, tiled=True)


def step(
    conc,
    porosity,
    cell_cond,
    soil_class,
    active,
    class_cond,
    sorb_affinity,
    sorb_capacity,
    surf_conc,
    surf_rate,
    surf_group,
    surf_local,
):
    groups = lax.axis_size("grp")
    owners = lax.axis_size("col")
    comps, depth, width = conc.shape
    n = surf_conc.shape[1]
    sds = jax.ShapeDtypeStruct
    first = (lax.axis_index("col") * depth).astype(jnp.int32).reshape(1)

    meta = pl.pallas_call(
        meta_kernel,
        out_shape=sds((owners, 2, LANES), jnp.int32),
        in_specs=[full()] * 2,
        out_specs=full(),
        interpret=INTERPRET,
        compiler_params=pltpu.CompilerParams(vmem_limit_bytes=24 << 20),
        name="meta",
    )(far(soil_class.reshape(1, LANES)), far(active.reshape(1, LANES)))
    meta = exchange(meta, "col")

    rate = surf_rate.reshape(1, n)
    group = surf_group.reshape(1, n)
    local = surf_local.reshape(1, n)
    smem = pl.BlockSpec(memory_space=pltpu.SMEM)
    me = lax.axis_index("grp").astype(jnp.int32).reshape(1)
    masks = halvings(groups)
    keep, surf_send, *brick = pl.pallas_call(
        surf_pack_kernel,
        out_shape=(
            sds((groups // 2, 16, LANES), F32),
            sds((groups // 2, 16, LANES), F32),
            held((comps, depth, width)),
            held((depth, width)),
            held((depth, width)),
        ),
        in_specs=[smem] + [full()] * 4 + [pl.BlockSpec(memory_space=HBM)] * 3,
        out_specs=tuple(full() for _ in range(5)),
        scratch_shapes=[
            pltpu.VMEM((3, 16 * groups, n), jnp.bfloat16),
            pltpu.SemaphoreType.DMA((3,)),
        ],
        interpret=INTERPRET,
        compiler_params=pltpu.CompilerParams(vmem_limit_bytes=24 << 20),
        name="surf_pack",
    )(
        me,
        *(far(x) for x in (surf_conc, rate, group, local)),
        *(far(x) for x in (conc, porosity, cell_cond)),
    )
    surf_parts = [keep]
    for k, (mask, partner) in enumerate(zip(masks, partners(groups))):
        if k:
            surf_send = sum(x[mask : 2 * mask] for x in surf_parts)
        surf_parts.append(swap(surf_send, partner))
    surf_parts = [x[:1] for x in surf_parts]

    send, g, vw = pl.pallas_call(
        eliminate_kernel,
        out_shape=(
            held((owners * ROWS, LANES)),
            held((comps, depth, width)),
            held((2, depth, width)),
        ),
        in_specs=[smem, smem] + [full()] * 4,
        out_specs=(full(), full(), full()),
        interpret=INTERPRET,
        compiler_params=pltpu.CompilerParams(vmem_limit_bytes=24 << 20),
        input_output_aliases={2: 1},
        name="eliminate",
    )(first, far(class_cond), *(near(x) for x in brick), near(meta))
    recv = exchange(send.reshape(owners, ROWS, 1, LANES), "col")

    table = jnp.concatenate(
        [sorb_affinity.T, sorb_capacity[None], jnp.zeros((15 - comps, 16), F32)], axis=0
    )
    sorb = call(lookup_kernel, held((owners, 16, LANES)), 2, name="lookup")(table, meta)

    ends, top = call(
        interface_kernel,
        (held((owners * 24, LANES)), held((1, 16, LANES))),
        2 + len(surf_parts),
        name="interface",
    )(recv.reshape(owners * ROWS, LANES), active.reshape(1, LANES), *surf_parts)
    ends = exchange(ends.reshape(owners, 24, LANES), "col")
    for k, mask in enumerate(doublings(groups)):
        if k:
            top = jnp.concatenate([top, other], axis=0)
        other = swap(top, mask)

    log_free = pl.pallas_call(
        speciate_kernel,
        out_shape=sds((comps, depth, width), F32),
        in_specs=[full()] * 5,
        out_specs=pl.BlockSpec(memory_space=pl.ANY),
        scratch_shapes=[
            pltpu.VMEM((comps, depth, width), F32),
            pltpu.SemaphoreType.DMA((CHUNKS,)),
        ],
        interpret=INTERPRET,
        compiler_params=pltpu.CompilerParams(vmem_limit_bytes=24 << 20),
        name="speciate",
    )(near(g), near(vw), near(porosity), near(ends), near(sorb))

    flux = pl.pallas_call(
        surf_flux_kernel,
        out_shape=sds((comps, n), F32),
        in_specs=[smem] + [full()] * 6,
        out_specs=full(),
        interpret=INTERPRET,
        compiler_params=pltpu.CompilerParams(vmem_limit_bytes=24 << 20),
        name="surf_flux",
    )(me, near(top), near(other), *(near(x) for x in (surf_conc, rate, group, local)))
    return (log_free, flux)


def solution(mesh):
    return jax.shard_map(
        step,
        mesh=mesh,
        in_specs=(
            P(None, "col", "grp"),
            P("col", "grp"),
            P("col", "grp"),
            P(("grp", "col")),
            P(("grp", "col")),
            P(),
            P(),
            P(),
            P(None, ("grp", "col")),
            P(("grp", "col")),
            P(("grp", "col"), None),
            P(("grp", "col")),
        ),
        out_specs=(P(None, "col", "grp"), P(None, ("grp", "col"))),
        check_vma=False,
    )
```
